32 devices in a mesh: seq: 8 (over z, y), win: 4 (over x, core).
Axes of the slice: x: 2, y: 2, z: 4, core: 2. Of those that a mesh axis runs over, the one named last changes fastest.
Arguments:
- queries: bfloat16 [4096, 1024], P(('win', 'seq')), parts along dimension 0, may hold values from -6 to 6
- key_rows: bfloat16 [4096, 1024], P(('win', 'seq')), parts along dimension 0, may hold values from -6 to 6
- value_rows: bfloat16 [4096, 2048], P(('win', 'seq')), parts along dimension 0, may hold values from -6 to 6
- residual: bfloat16 [4096, 1024], P(('win', 'seq')), parts along dimension 0, may hold values from -6 to 6
- out_weight: bfloat16 [2048, 1024], P(None, 'seq'), may hold values from -0.125 to 0.125
- expert_in: bfloat16 [8, 1024, 768], P('seq'), may hold values from -0.1875 to 0.1875
- expert_out: bfloat16 [8, 384, 1024], P('seq'), may hold values from -0.3125 to 0.3125
- expert_ids: int32 [4096, 2], P(('win', 'seq')), parts along dimension 0, may hold values from 0 to 7, all different within a row; in each aligned block of 128 rows (0 to 127, 128 to 255, ...) at most 64 rows name the same one
- gate_values: float32 [4096, 2], P(('win', 'seq')), parts along dimension 0, may hold values from 0.2 to 1
Outputs:
- layer_out: bfloat16 [4096, 1024], P(('win', 'seq')), parts along dimension 0
The draws below stay inside these ranges and needn't reach their ends.
There are 4 independent parts, one for each index of `win`. The reference program is written for one: setup_inputs(seed, part) draws one part's arguments, and reference() takes and returns one part's arrays. A program takes and returns all parts, laid end to end along the dimension named above; an argument that names none is the same for every part. Nothing has to cross between parts.
Inputs may be any that keep to these rules, and one draw needn't show every extreme that they name: `expert_ids`: the 2 ids of a row differ. Within the rows of one block of 128 tokens no expert is named by more than 64 rows, a bound that some block reaches. Every expert is named somewhere.
All inputs are finite; a program needn't handle non-finite values.
Results may differ from the reference program's by a relative error of at most 0.013.
Values may be sent and summed in bfloat16 or wider, within the bound.
No kernel may reach another device: no remote copies, remote signals or barrier semaphores. Data moves between devices by JAX's collectives and lax.ppermute only.
A program may use at most 128 MiB of HBM per device.

```python
import math
import jax
import jax.numpy as jnp
import numpy as np
from jax import lax

D = 1024
H = 16
DK = 64
DV = 128
HE = 384
TOP = 2
TOK_DEV = 128
TOKENS = 1024
EXPERTS = 8
CAP = 64
N_SEQ = 8


def block_levels(key, dims, shards, low, top_value):
    gain, own = 1.0, jax.random.fold_in(key, 6)
    for dim, blocks in shards:
        draws = jnp.exp(jax.random.uniform(jax.random.fold_in(own, dim), (blocks,), jnp.float32, low / len(shards), top_value / len(shards)))
        gain = gain * jnp.repeat(draws, dims[dim] // blocks).reshape([-1 if axis == dim else 1 for axis in range(len(dims))])
    return gain


def deal_out(own_key, own, number, rows, amount, top, most, skew):
    ranking = jax.random.permutation(own_key, amount)
    packed, common = load_shares(amount, rows * top, most, skew, True), load_shares(amount, rows * top, most, skew, False)
    places = jnp.arange(amount)

    def named(tallies, turn):
        used = int((tallies > 0).sum())
        fixed = max(1, used // 4)
        moved = fixed + (places - fixed + turn * (used - fixed)) % max(1, amount - fixed)
        return jnp.zeros((amount,), jnp.int32).at[ranking[jnp.where(places < fixed, places, moved)]].set(jnp.asarray(tallies, jnp.int32))

    tallies = jnp.where(number % 4 == 0, named(packed, number // 4), named(common, number - number // 4 - 1))
    mixed = jax.random.permutation(jax.random.fold_in(own, 3), amount)
    giver, sink = mixed[0:amount // 2 * 2:2], mixed[1:amount // 2 * 2:2]
    slack = jnp.minimum(tallies[giver] - 1, most - tallies[sink]) // 2
    slack = jnp.where((giver == ranking[0]) | (sink == ranking[0]) | (tallies[sink] == 0), 0, jnp.maximum(slack, 0))
    moved = jax.random.randint(jax.random.fold_in(own, 4), (amount // 2,), 0, 1 << 20) % (slack + 1)
    tallies = tallies.at[giver].add(-moved).at[sink].add(moved)
    labels = jnp.searchsorted(jnp.cumsum(tallies), jnp.arange(rows * top), side="right").astype(jnp.int32)
    grid = labels.reshape(top, rows).T
    grid = grid[jax.random.permutation(jax.random.fold_in(own, 1), rows)]
    turn = jax.random.randint(jax.random.fold_in(own, 2), (rows, 1), 0, top)
    return jnp.take_along_axis(grid, (jnp.arange(top)[None, :] + turn) % top, axis=1)


def load_shares(count, total, bound, skew, full):
    portions = [(1 << 20) // math.isqrt(rank ** skew) + 1 for rank in range(1, count + 1)]
    largest = bound if full else min(bound, max(-(-total // count), total * portions[0] // sum(portions)))
    least = 1 if total - largest >= count - 1 else 0
    counts, spare = [largest] + [least] * (count - 1), total - largest - least * (count - 1)
    while spare > 0:
        candidates = [i for i in range(1, count) if counts[i] < largest] or [i for i in range(1, count) if counts[i] < bound]
        mass, left = sum([portions[i] for i in candidates]), spare
        for i in candidates:
            extra = min(bound - counts[i], max(1, left * portions[i] // mass), spare)
            counts[i] = counts[i] + extra
            spare = spare - extra
    return np.array(counts)


def bell_draw(key, extent, width, most, pieces=(), held_as=jnp.bfloat16):
    drawn = jax.random.normal(key, extent, jnp.float32) * width
    if len(pieces) > 0:
        drawn = block_levels(key, extent, pieces, -0.22, 0.18) * drawn
    return jnp.clip(drawn, min=-most, max=most).astype(held_as)


def setup_inputs(seed: int = 0, part: int = 0) -> dict:
    splits = jax.random.split(jax.random.key(seed), 10)
    part_splits = jax.random.split(jax.random.fold_in(splits[9], part), 10)
    queries = bell_draw(part_splits[0], (TOKENS, H * DK), 1.0, 6.0, ((0, 8),))
    key_rows = bell_draw(part_splits[1], (TOKENS, H * DK), 1.0, 6.0, ((0, 8),))
    value_rows = bell_draw(part_splits[2], (TOKENS, H * DV), 1.0, 6.0, ((0, 8),))
    residual = bell_draw(part_splits[3], (TOKENS, D), 1.0, 6.0, ((0, 8),))
    out_weight = bell_draw(splits[4], (H * DV, D), (H * DV) ** -0.5, 0.125, ((1, 8),))
    expert_in = bell_draw(splits[5], (EXPERTS, D, 2 * HE), D ** -0.5, 0.1875, ((0, 8),))
    expert_out = bell_draw(splits[6], (EXPERTS, HE, D), HE ** -0.5, 0.3125, ((0, 8),))
    expert_ids_keys = jax.random.split(jax.random.fold_in(part_splits[7], 1), TOKENS // TOK_DEV)
    expert_ids_turns = jax.random.permutation(jax.random.fold_in(part_splits[7], 3), TOKENS // TOK_DEV)
    expert_ids = jax.vmap(lambda own, number: deal_out(jax.random.fold_in(part_splits[7], 2), own, number, TOK_DEV, EXPERTS, TOP, CAP, 2))(expert_ids_keys, expert_ids_turns).reshape((TOKENS, TOP))
    gate_values = jnp.clip(0.2 + 0.8 * jax.random.uniform(part_splits[8], (TOKENS, TOP), jnp.float32) ** block_levels(part_splits[8], (TOKENS, TOP), ((0, 8),), -0.2, 0.2), 0.2, 1.0)
    return dict(queries=queries, key_rows=key_rows, value_rows=value_rows, residual=residual, out_weight=out_weight, expert_in=expert_in, expert_out=expert_out, expert_ids=expert_ids, gate_values=gate_values)


def reference(queries, key_rows, value_rows, residual, out_weight, expert_in, expert_out, expert_ids, gate_values):
    q_blocks = queries.reshape(N_SEQ, TOK_DEV, H, DK)
    k_blocks = key_rows.reshape(N_SEQ, TOK_DEV, H, DK)
    v_blocks = value_rows.reshape(N_SEQ, TOK_DEV, H, DV)
    causal = jnp.arange(TOK_DEV)[:, None] >= jnp.arange(TOK_DEV)[None, :]
    starts = jnp.arange(N_SEQ).astype(jnp.float32) * TOK_DEV

    def block_step(carried, block_in):
        q_block, k_block, v_block, start_pos = block_in
        q_float = q_block.astype(jnp.float32)
        k_float = k_block.astype(jnp.float32)
        v_float = v_block.astype(jnp.float32)
        scores = jnp.einsum('thd,shd->hts', q_float, k_float)
        scores = jnp.where(causal[None], scores, 0.0).astype(jnp.bfloat16)
        scores = lax.optimization_barrier(scores).astype(jnp.float32)
        intra_sum = jnp.einsum('hts,she->the', scores, v_float)
        inter_sum = jnp.einsum('thd,hde->the', q_float, carried, precision=lax.Precision.HIGHEST)
        position = start_pos + jnp.arange(TOK_DEV).astype(jnp.float32)
        scaling = lax.rsqrt((position + 1.0) * DK)
        produced = ((intra_sum + inter_sum) * scaling[:, None, None]).astype(jnp.bfloat16)
        carried = carried + jnp.einsum('thd,the->hde', k_float, v_float)
        return (carried, produced)
    _, attended = lax.scan(block_step, jnp.zeros((H, DK, DV), jnp.float32), (q_blocks, k_blocks, v_blocks, starts))
    attended = attended.reshape(TOKENS, H * DV)
    projected = jnp.dot(attended, out_weight, preferred_element_type=jnp.float32)
    hidden = (residual.astype(jnp.float32) + projected).astype(jnp.bfloat16)
    hidden_float = hidden.astype(jnp.float32)
    normed = (hidden_float * lax.rsqrt(lax.optimization_barrier(jnp.mean(hidden_float * hidden_float, axis=-1, keepdims=True)) + 1e-06)).astype(jnp.bfloat16)
    ids_block = expert_ids.reshape(N_SEQ, TOK_DEV * TOP)
    one_hot = (ids_block[..., None] == jnp.arange(EXPERTS)[None, None, :]).astype(jnp.int32)
    earlier = jnp.cumsum(one_hot, axis=1) - one_hot
    slot_index = lax.optimization_barrier(jnp.sum(earlier * one_hot, axis=-1))
    block_of = jnp.arange(N_SEQ)[:, None].astype(jnp.int32)
    dest_row = (ids_block * (N_SEQ * CAP) + block_of * CAP + slot_index).reshape(-1).astype(jnp.int32)
    sources = jnp.repeat(normed, TOP, axis=0)
    buffer = jnp.zeros((EXPERTS * N_SEQ * CAP, D), jnp.bfloat16).at[dest_row].set(sources)
    buffer = buffer.reshape(EXPERTS, N_SEQ * CAP, D)

    def run_expert(item):
        rows_in, weight_in, weight_out = item
        act = jnp.dot(rows_in, weight_in, preferred_element_type=jnp.float32)
        inner = (jax.nn.silu(act[:, :HE]) * act[:, HE:]).astype(jnp.bfloat16)
        return jnp.dot(inner, weight_out, preferred_element_type=jnp.float32).astype(jnp.bfloat16)
    expert_rows = lax.map(run_expert, (buffer, expert_in, expert_out))
    picked = expert_rows.reshape(EXPERTS * N_SEQ * CAP, D)[dest_row]
    combined = lax.optimization_barrier(jnp.sum(picked.astype(jnp.float32).reshape(TOKENS, TOP, D) * gate_values[:, :, None], axis=1))
    return (hidden_float + combined).astype(jnp.bfloat16)
```

```python
import functools

import jax
import jax.numpy as jnp
from jax import lax
from jax.experimental import pallas as pl
from jax.experimental.pallas import tpu as pltpu
from jax.sharding import PartitionSpec as P

D = 1024
H = 16
DK = 64
DV = 128
HE = 384
TOP = 2
UNROLL_LIMIT = 16
BF = jnp.bfloat16
F32 = jnp.float32
VMEM = pl.BlockSpec(memory_space=pltpu.VMEM)


def call(body, outs, n_in, scratch=(), name=None):
    return pl.pallas_call(
        body,
        out_shape=outs,
        in_specs=[VMEM] * n_in,
        out_specs=jax.tree.map(lambda _: VMEM, outs),
        scratch_shapes=scratch,
        name=name,
    )


def sds(shape, dtype):
    return jax.ShapeDtypeStruct(shape, dtype)


def dot(a, b, dims=((1,), (0,))):
    return lax.dot_general(a, b, (dims, ((), ())), preferred_element_type=F32)


def states_body(k_ref, v_ref, mine_ref, send_ref, full):
    half = full.shape[0] // 2
    for p in range(H // 2):
        r = dot(k_ref[:, 2 * DK * p : 2 * DK * (p + 1)], v_ref[:, 2 * DV * p : 2 * DV * (p + 1)], ((0,), (0,)))
        full[2 * DK * p : 2 * DK * p + DK, :] = r[:DK, :DV]
        full[2 * DK * p + DK : 2 * DK * (p + 1), :] = r[DK:, DV:]
    y = lax.rem(lax.axis_index("seq"), 2)
    mine_ref[...] = full[pl.ds(pl.multiple_of(y * half, half), half), :]
    send_ref[...] = full[pl.ds(pl.multiple_of((1 - y) * half, half), half), :].astype(BF)


def intra_body(q_ref, k_ref, v_ref, out_ref):
    length = q_ref.shape[0]
    lane = lax.broadcasted_iota(jnp.int32, (length, 2 * DK), 1)
    row = lax.broadcasted_iota(jnp.int32, (length, length), 0)
    col = lax.broadcasted_iota(jnp.int32, (length, length), 1)
    causal = row >= col
    for p in range(H // 2):
        q = q_ref[:, 2 * DK * p : 2 * DK * (p + 1)]
        k = k_ref[:, 2 * DK * p : 2 * DK * (p + 1)]
        for i in range(2):
            mine = (lane < DK) if i == 0 else (lane >= DK)
            s = dot(jnp.where(mine, q, jnp.zeros_like(q)), k, ((1,), (1,)))
            s = jnp.where(causal, s, 0.0).astype(BF)
            c = (2 * p + i) * DV
            out_ref[:, c : c + DV] = dot(s, v_ref[:, c : c + DV])


def keys_of(meta, experts):
    length = meta.shape[1]
    e = lax.broadcasted_iota(jnp.int32, (experts, length), 0).astype(F32)
    first, second = meta[0:1, :] == e, meta[1:2, :] == e
    named = jnp.logical_or(first, second)
    a = lax.broadcasted_iota(jnp.int32, (length, length), 0)
    b = lax.broadcasted_iota(jnp.int32, (length, length), 1)
    before = jnp.where(a < b, 1.0, 0.0).astype(BF)
    count = dot(jnp.where(named, 1.0, 0.0).astype(BF), before)
    key = jnp.where(named, count, -1.0)
    gate = jnp.where(first, meta[2:3, :], jnp.where(second, meta[3:4, :], 0.0))
    return key, gate


def deal(key_ref, normed, outs, cap):
    s = lax.axis_index("seq")
    length = normed.shape[0]
    c = lax.broadcasted_iota(jnp.int32, (cap, length), 0).astype(F32)
    picks = [
        jnp.where(c == key_ref[pl.ds(jnp.bitwise_xor(s, k), 1), :], 1.0, 0.0).astype(BF)
        for k in range(len(outs))
    ]
    rows = dot(jnp.concatenate(picks, axis=0), normed).astype(BF)
    for k, out in enumerate(outs):
        out[...] = rows[k * cap : (k + 1) * cap, :]


def project_body(n, q_ref, intra_ref, pm_ref, po_ref, wown_ref, res_ref, meta_ref, *refs):
    fwd, bwd = n // 2, n // 2 - 1
    pieces, refs = refs[: 2 * (fwd + bwd)], refs[2 * (fwd + bwd) :]
    fm, refs_f = pieces[:fwd], pieces[fwd : 2 * fwd]
    bm, refs_b = pieces[2 * fwd : 2 * fwd + bwd], pieces[2 * fwd + bwd :]
    hidden_ref, normed_ref = refs[:2]
    outs = refs[2 : 2 + n // 2]
    prefix, att, hid, key_ref = refs[2 + n // 2 :]
    s = lax.axis_index("seq")
    c = lax.rem(lax.axis_index("win"), 2)
    y = lax.rem(s, 2)
    length = q_ref.shape[0]
    half = prefix.shape[0] // 2
    prefix[pl.ds(pl.multiple_of(y * half, half), half), :] = pm_ref[...]
    prefix[pl.ds(pl.multiple_of((1 - y) * half, half), half), :] = po_ref[...]
    place = (s * length + lax.broadcasted_iota(jnp.int32, (length, 1), 0)).astype(F32)
    scaling = lax.rsqrt((place + 1.0) * DK)
    zero = jnp.zeros((DK, DV), BF)
    for p in range(H // 2):
        top = jnp.concatenate([prefix[2 * DK * p : 2 * DK * p + DK, :], zero], axis=1)
        low = jnp.concatenate([zero, prefix[2 * DK * p + DK : 2 * DK * (p + 1), :]], axis=1)
        inter = dot(q_ref[:, 2 * DK * p : 2 * DK * (p + 1)], jnp.concatenate([top, low], axis=0))
        cols = slice(2 * DV * p, 2 * DV * (p + 1))
        att[:, cols] = ((intra_ref[:, cols] + inter) * scaling).astype(BF)
    rows = att.shape[1] // 2
    width = wown_ref.shape[1]
    att_m = att[:, pl.ds(pl.multiple_of(c * rows, rows), rows)]
    att_p = att[:, pl.ds(pl.multiple_of((1 - c) * rows, rows), rows)]
    pos = jnp.where(y == 0, s // 2, n - 1 - s // 2)

    def source(shift):
        at = lax.rem(pos + shift + n, n)
        return jnp.where(at < n // 2, 2 * at, 2 * (n - 1 - at) + 1)

    def put(shift, value):
        hid[:, pl.ds(pl.multiple_of(source(shift) * width, width), width)] = value

    put(0, dot(att[...], wown_ref[...]))
    for j in range(fwd):
        if j < bwd:
            m = jnp.concatenate([fm[j][...], bm[j][...]], axis=1)
            o = jnp.concatenate([refs_f[j][...], refs_b[j][...]], axis=1)
            both = dot(att_m, m) + dot(att_p, o)
            put(-(j + 1), both[:, :width])
            put(j + 1, both[:, width:])
        else:
            put(-(j + 1), dot(att_m, fm[j][...]) + dot(att_p, refs_f[j][...]))
    hidden = (res_ref[...].astype(F32) + hid[...]).astype(BF)
    hidden_ref[...] = hidden
    h = hidden.astype(F32)
    normed = (h * lax.rsqrt(jnp.mean(h * h, axis=-1, keepdims=True) + 1e-06)).astype(BF)
    normed_ref[...] = normed
    key_ref[...] = keys_of(meta_ref[...], n)[0]
    deal(key_ref, normed, outs, outs[0].shape[0])


def deal_body(n, normed_ref, meta_ref, *refs):
    outs, key_ref = refs[:-1], refs[-1]
    key_ref[...] = keys_of(meta_ref[...], n)[0]
    deal(key_ref, normed_ref[...], outs, outs[0].shape[0])


def expert_body(parts, win_ref, wout_ref, *refs):
    ins, outs = refs[:parts], refs[parts:]
    cap = ins[0].shape[0]
    x = jnp.concatenate([r[...] for r in ins], axis=0)
    act = dot(x, win_ref[0])
    gate = act[:, :HE]
    inner = (gate / (1.0 + jnp.exp(-gate)) * act[:, HE:]).astype(BF)
    rows = dot(inner, wout_ref[0]).astype(BF)
    for k in range(parts):
        outs[k][...] = rows[k * cap : (k + 1) * cap, :]


def gather_rows(n, meta, ins, key_ref, gate_ref):
    key, gate = keys_of(meta, n)
    key_ref[...] = key
    gate_ref[...] = gate
    s = lax.axis_index("seq")
    cap = ins[0].shape[0]
    length = meta.shape[1]
    c = lax.broadcasted_iota(jnp.int32, (cap, length), 0).astype(F32)
    high, low = [], []
    for k in range(len(ins)):
        e = pl.ds(jnp.bitwise_xor(s, k), 1)
        w = jnp.where(c == key_ref[e, :], gate_ref[e, :], 0.0)
        h = w.astype(BF)
        high.append(h)
        low.append((w - h.astype(F32)).astype(BF))
    rows = jnp.concatenate([r[...] for r in ins], axis=0)
    dims = ((0,), (0,))
    return dot(jnp.concatenate(high, axis=0), rows, dims) + dot(jnp.concatenate(low, axis=0), rows, dims)


def partial_body(n, meta_ref, *refs):
    ins, out_ref, key_ref, gate_ref = refs[:-3], refs[-3], refs[-2], refs[-1]
    out_ref[...] = gather_rows(n, meta_ref[...], ins, key_ref, gate_ref).astype(BF)


def final_body(n, meta_ref, hidden_ref, other_ref, *refs):
    ins, out_ref, key_ref, gate_ref = refs[:-3], refs[-3], refs[-2], refs[-1]
    total = gather_rows(n, meta_ref[...], ins, key_ref, gate_ref)
    total = total + other_ref[...].astype(F32) + hidden_ref[...].astype(F32)
    out_ref[...] = total.astype(BF)


def small_group(
    queries,
    key_rows,
    value_rows,
    residual,
    out_weight,
    expert_in,
    expert_out,
    expert_ids,
    gate_values,
):
    n = lax.axis_size("seq")
    length = queries.shape[0]
    s = lax.axis_index("seq")
    c = lax.rem(lax.axis_index("win"), 2)
    y = lax.rem(s, 2)
    near = n // 2
    cap = max(2, 2 * length * TOP // n)
    half = H * DK // 2
    order = [2 * i for i in range(n // 2)] + [2 * i + 1 for i in reversed(range(n // 2))]
    ahead = [(order[i], order[(i + 1) % n]) for i in range(n)]
    back = [(b, a) for a, b in ahead]

    def flip(x, k):
        return lax.ppermute(x, "seq", [(i, i ^ k) for i in range(n)])

    def swap_core(x):
        return lax.ppermute(x, "win", [(i, i ^ 1) for i in range(lax.axis_size("win"))])

    mine, sent = call(
        states_body,
        (sds((half, DV), F32), sds((half, DV), BF)),
        2,
        [pltpu.VMEM((2 * half, DV), F32)],
        name="states",
    )(key_rows, value_rows)
    got = flip(sent, 1).astype(F32)
    run = mine + got
    before = jnp.zeros_like(mine)
    step = 1
    while step < n // 2:
        hop = [(i, i + 2 * step) for i in range(n - 2 * step)]
        came = lax.ppermute(run.astype(BF), "seq", hop).astype(F32)
        before, run = before + came, run + came
        step *= 2
    prefix_mine = (before + jnp.where(y == 0, 0.0, got)).astype(BF)
    prefix_other = flip((before + jnp.where(y == 0, mine, 0.0)).astype(BF), 1)

    rows = H * DV // 2
    piece = lax.dynamic_slice_in_dim(out_weight, c * rows, rows, 0)
    fm, bm = [], []
    f = b = piece
    for j in range(near):
        f = lax.ppermute(f, "seq", ahead)
        fm.append(f)
        if j < near - 1:
            b = lax.ppermute(b, "seq", back)
            bm.append(b)
    fp = [swap_core(x) for x in fm]
    bp = [swap_core(x) for x in bm]

    meta = jnp.concatenate([expert_ids.astype(F32), gate_values], axis=1).T
    meta_far = flip(meta, near)

    intra = call(intra_body, sds((length, H * DV), F32), 3, name="intra")(queries, key_rows, value_rows)

    ins = [queries, intra, prefix_mine, prefix_other, out_weight, residual, meta, *fm, *fp, *bm, *bp]
    row_buf = sds((cap, D), BF)
    hidden, normed, *deal_own = call(
        functools.partial(project_body, n),
        (sds((length, D), BF), sds((length, D), BF), *[row_buf] * near),
        len(ins),
        [
            pltpu.VMEM((2 * half, DV), BF),
            pltpu.VMEM((length, H * DV), BF),
            pltpu.VMEM((length, D), F32),
            pltpu.VMEM((n, length), F32),
        ],
        name="project",
    )(*ins)
    normed_far = flip(normed, near)
    own_in = [deal_own[0]] + [flip(deal_own[k], k) for k in range(1, near)]
    deal_far = call(
        functools.partial(deal_body, n),
        tuple([row_buf] * near),
        2,
        [pltpu.VMEM((n, length), F32)],
        name="deal",
    )(normed_far, meta_far)
    far_in = [deal_far[0]] + [flip(deal_far[k], k) for k in range(1, near)]

    experts = call(
        functools.partial(expert_body, near), tuple([row_buf] * near), 2 + near, name="experts"
    )
    own_out = experts(expert_in, expert_out, *own_in)
    far_out = experts(expert_in, expert_out, *far_in)
    own_back = [own_out[0]] + [flip(own_out[k], k) for k in range(1, near)]
    far_back = [far_out[0]] + [flip(far_out[k], k) for k in range(1, near)]
    scratch = [pltpu.VMEM((n, length), F32), pltpu.VMEM((n, length), F32)]
    part_far = call(
        functools.partial(partial_body, n), sds((length, D), BF), 1 + near, scratch, name="partial"
    )(meta_far, *far_back)
    part_own = flip(part_far, near)
    return call(
        functools.partial(final_body, n), sds((length, D), BF), 3 + near, scratch, name="final"
    )(meta, hidden, part_own, *own_back)


def large_group(
    queries,
    key_rows,
    value_rows,
    residual,
    out_weight,
    expert_in,
    expert_out,
    expert_ids,
    gate_values,
):
    length = queries.shape[0]
    q_heads = queries.reshape(length, H, DK)
    k_heads = key_rows.reshape(length, H, DK)
    v_heads = value_rows.reshape(length, H, DV)
    local_state = jnp.einsum("thd,the->hde", k_heads, v_heads, preferred_element_type=F32)
    gathered = lax.all_gather(local_state.astype(BF), "seq")
    prefix = lax.fori_loop(
        0,
        lax.axis_index("seq"),
        lambda i, total: total + lax.dynamic_index_in_dim(gathered, i, 0, False).astype(F32),
        jnp.zeros_like(local_state),
    )
    causal = jnp.arange(length)[:, None] >= jnp.arange(length)[None, :]
    scores = jnp.einsum("thd,shd->hts", q_heads, k_heads, preferred_element_type=F32)
    scores = jnp.where(causal[None], scores, 0.0).astype(BF)
    intra_sum = jnp.einsum("hts,she->the", scores, v_heads, preferred_element_type=F32)
    inter_sum = jnp.einsum(
        "thd,hde->the", q_heads.astype(F32), prefix, precision=lax.Precision.HIGHEST
    )
    position = (lax.axis_index("seq") * length + jnp.arange(length)).astype(F32)
    scaling = lax.rsqrt((position + 1.0) * DK)
    attended = ((intra_sum + inter_sum) * scaling[:, None, None]).astype(BF).reshape(length, H * DV)
    projected = jnp.dot(
        attended,
        lax.all_gather(out_weight, "seq", axis=1, tiled=True),
        preferred_element_type=F32,
    )
    hidden = (residual.astype(F32) + projected).astype(BF)
    hidden_float = hidden.astype(F32)
    normed = (
        hidden_float
        * lax.rsqrt(jnp.mean(hidden_float * hidden_float, axis=-1, keepdims=True) + 1e-06)
    ).astype(BF)
    experts = lax.axis_size("seq") * expert_in.shape[0]
    capacity = max(2, 2 * length * TOP // experts)
    flat_ids = expert_ids.reshape(-1)
    one_hot = (flat_ids[:, None] == jnp.arange(experts)[None, :]).astype(jnp.int32)
    earlier = jnp.cumsum(one_hot, axis=0) - one_hot
    slot_index = jnp.sum(earlier * one_hot, axis=-1)
    dest_row = flat_ids * capacity + slot_index
    buffer = (
        jnp.zeros((experts * capacity, D), BF).at[dest_row].set(jnp.repeat(normed, TOP, axis=0))
    )
    buffer = buffer.reshape(experts, 1, capacity, D)
    act = jnp.einsum(
        "ensd,edf->ensf",
        lax.all_to_all(buffer, "seq", split_axis=0, concat_axis=1, tiled=True),
        expert_in,
        preferred_element_type=F32,
    )
    inner = (jax.nn.silu(act[..., :HE]) * act[..., HE:]).astype(BF)
    produced_all = jnp.einsum(
        "ensf,efd->ensd", inner, expert_out, preferred_element_type=F32
    ).astype(BF)
    returned_rows = lax.all_to_all(produced_all, "seq", split_axis=1, concat_axis=0, tiled=True)
    picked = returned_rows.reshape(experts * capacity, D)[dest_row]
    combined = jnp.sum(
        picked.astype(F32).reshape(length, TOP, D) * gate_values[:, :, None], axis=1
    )
    return (hidden_float + combined).astype(BF)


def solution(mesh):
    n = mesh.shape["seq"]
    even_win = mesh.shape["win"] % 2 == 0
    small = 4 <= n <= UNROLL_LIMIT and n & (n - 1) == 0 and even_win
    in_specs = (
        P(("win", "seq"), None),
        P(("win", "seq"), None),
        P(("win", "seq"), None),
        P(("win", "seq"), None),
        P(None, "seq"),
        P("seq", None, None),
        P("seq", None, None),
        P(("win", "seq"), None),
        P(("win", "seq"), None),
    )
    out_specs = P(("win", "seq"), None)
    return jax.shard_map(
        small_group if small else large_group,
        mesh=mesh,
        in_specs=in_specs,
        out_specs=out_specs,
        check_vma=False,
    )
```

```python
import functools

import jax
import jax.numpy as jnp
from jax import lax
from jax.experimental import pallas as pl
from jax.experimental.pallas import tpu as pltpu
from jax.sharding import PartitionSpec as P


D = 1024
H = 16
DK = 64
DV = 128
HE = 384
TOP = 2
UNROLL_LIMIT = 16
KERNEL_VMEM = 24 * 1024 * 1024
BF = jnp.bfloat16
F32 = jnp.float32
VMEM = pl.BlockSpec(memory_space=pltpu.VMEM)


def call(body, outs, n_in, scratch=()):
    run = pl.pallas_call(
        body,
        out_shape=outs,
        in_specs=[VMEM] * n_in,
        out_specs=jax.tree.map(lambda _: VMEM, outs),
        scratch_shapes=scratch,
        compiler_params=pltpu.CompilerParams(vmem_limit_bytes=KERNEL_VMEM),
    )
    return lambda *xs: run(*[pltpu.with_memory_space_constraint(x, pltpu.VMEM) for x in xs])


def sds(shape, dtype):
    return pltpu.VMEM(shape, dtype)


def dot(a, b, dims=((1,), (0,))):
    return lax.dot_general(a, b, (dims, ((), ())), preferred_element_type=F32)


def states_body(k_ref, v_ref, mine_ref, send_ref, full):
    half = full.shape[0] // 2
    for p in range(H // 2):
        r = dot(k_ref[:, 2 * DK * p : 2 * DK * (p + 1)], v_ref[:, 2 * DV * p : 2 * DV * (p + 1)], ((0,), (0,)))
        full[2 * DK * p : 2 * DK * p + DK, :] = r[:DK, :DV]
        full[2 * DK * p + DK : 2 * DK * (p + 1), :] = r[DK:, DV:]
    y = lax.rem(lax.axis_index("seq"), 2)
    mine_ref[...] = full[pl.ds(pl.multiple_of(y * half, half), half), :]
    send_ref[...] = full[pl.ds(pl.multiple_of((1 - y) * half, half), half), :].astype(BF)


def intra_body(first, q_ref, k_ref, v_ref, out_ref):
    length = q_ref.shape[0]
    lane = lax.broadcasted_iota(jnp.int32, (length, 2 * DK), 1)
    row = lax.broadcasted_iota(jnp.int32, (length, length), 0)
    col = lax.broadcasted_iota(jnp.int32, (length, length), 1)
    causal = row >= col
    for p in range(first, first + H // 4):
        q = q_ref[:, 2 * DK * p : 2 * DK * (p + 1)]
        k = k_ref[:, 2 * DK * p : 2 * DK * (p + 1)]
        for i in range(2):
            mine = (lane < DK) if i == 0 else (lane >= DK)
            s = dot(jnp.where(mine, q, jnp.zeros_like(q)), k, ((1,), (1,)))
            s = jnp.where(causal, s, 0.0).astype(BF)
            c = (2 * p + i) * DV
            o = c - 2 * first * DV
            out_ref[:, o : o + DV] = dot(s, v_ref[:, c : c + DV])


def keys_of(meta, experts):
    length = meta.shape[1]
    e = lax.broadcasted_iota(jnp.int32, (experts, length), 0).astype(F32)
    first, second = meta[0:1, :] == e, meta[1:2, :] == e
    named = jnp.logical_or(first, second)
    a = lax.broadcasted_iota(jnp.int32, (length, length), 0)
    b = lax.broadcasted_iota(jnp.int32, (length, length), 1)
    before = jnp.where(a < b, 1.0, 0.0).astype(BF)
    count = dot(jnp.where(named, 1.0, 0.0).astype(BF), before)
    key = jnp.where(named, count, -1.0)
    gate = jnp.where(first, meta[2:3, :], jnp.where(second, meta[3:4, :], 0.0))
    return key, gate


def deal(key_ref, normed, outs, cap):
    s = lax.axis_index("seq")
    length = normed.shape[0]
    c = lax.broadcasted_iota(jnp.int32, (cap, length), 0).astype(F32)
    picks = [
        jnp.where(c == key_ref[pl.ds(jnp.bitwise_xor(s, k), 1), :], 1.0, 0.0).astype(BF)
        for k in range(len(outs))
    ]
    rows = dot(jnp.concatenate(picks, axis=0), normed).astype(BF)
    for k, out in enumerate(outs):
        out[...] = rows[k * cap : (k + 1) * cap, :]


def project_body(n, offsets, q_ref, ia_ref, ib_ref, pm_ref, po_ref, wown_ref, res_ref, meta_ref, *refs):
    fwd, bwd = n // 2, n // 2 - 1
    copies = len(offsets)
    fs = [refs[j * copies : (j + 1) * copies] for j in range(fwd)]
    refs = refs[fwd * copies :]
    bs = [refs[j * copies : (j + 1) * copies] for j in range(bwd)]
    refs = refs[bwd * copies :]
    hidden_ref, normed_ref = refs[:2]
    outs = refs[2 : 2 + n // 2]
    prefix, att, hid, key_ref = refs[2 + n // 2 :]
    s = lax.axis_index("seq")
    w = lax.axis_index("win")
    y = lax.rem(s, 2)
    length = q_ref.shape[0]
    half = prefix.shape[0] // 2
    prefix[pl.ds(pl.multiple_of(y * half, half), half), :] = pm_ref[...]
    prefix[pl.ds(pl.multiple_of((1 - y) * half, half), half), :] = po_ref[...]
    place = (s * length + lax.broadcasted_iota(jnp.int32, (length, 1), 0)).astype(F32)
    scaling = lax.rsqrt((place + 1.0) * DK)
    zero = jnp.zeros((DK, DV), BF)
    for p in range(H // 2):
        top = jnp.concatenate([prefix[2 * DK * p : 2 * DK * p + DK, :], zero], axis=1)
        low = jnp.concatenate([zero, prefix[2 * DK * p + DK : 2 * DK * (p + 1), :]], axis=1)
        inter = dot(q_ref[:, 2 * DK * p : 2 * DK * (p + 1)], jnp.concatenate([top, low], axis=0))
        cols = slice(2 * DV * p, 2 * DV * (p + 1))
        src, at = (ia_ref, p) if p < H // 4 else (ib_ref, p - H // 4)
        intra = src[:, 2 * DV * at : 2 * DV * (at + 1)]
        att[:, cols] = ((intra + inter) * scaling).astype(BF)
    rows = att.shape[1] // copies
    width = wown_ref.shape[1]
    parts = [
        att[:, pl.ds(pl.multiple_of(jnp.bitwise_xor(w, o) * rows, rows), rows)] for o in offsets
    ]
    pos = jnp.where(y == 0, s // 2, n - 1 - s // 2)

    def source(shift):
        at = lax.rem(pos + shift + n, n)
        return jnp.where(at < n // 2, 2 * at, 2 * (n - 1 - at) + 1)

    def put(shift, value):
        hid[:, pl.ds(pl.multiple_of(source(shift) * width, width), width)] = value

    put(0, dot(att[...], wown_ref[...]))
    for j in range(fwd):
        both = j < bwd
        total = None
        for i, part in enumerate(parts):
            m = fs[j][i][...]
            if both:
                m = jnp.concatenate([m, bs[j][i][...]], axis=1)
            r = dot(part, m)
            total = r if total is None else total + r
        put(-(j + 1), total[:, :width])
        if both:
            put(j + 1, total[:, width:])
    hidden = (res_ref[...].astype(F32) + hid[...]).astype(BF)
    hidden_ref[...] = hidden
    h = hidden.astype(F32)
    normed = (h * lax.rsqrt(jnp.mean(h * h, axis=-1, keepdims=True) + 1e-06)).astype(BF)
    normed_ref[...] = normed
    key_ref[...] = keys_of(meta_ref[...], n)[0]
    deal(key_ref, normed, outs, outs[0].shape[0])


def deal_body(n, normed_ref, meta_ref, *refs):
    outs, key_ref = refs[:-1], refs[-1]
    key_ref[...] = keys_of(meta_ref[...], n)[0]
    deal(key_ref, normed_ref[...], outs, outs[0].shape[0])


def expert_body(parts, win_ref, wout_ref, *refs):
    ins, outs = refs[:parts], refs[parts:]
    cap = ins[0].shape[0]
    x = jnp.concatenate([r[...] for r in ins], axis=0)
    act = dot(x, win_ref[0])
    gate = act[:, :HE]
    inner = (gate / (1.0 + jnp.exp(-gate)) * act[:, HE:]).astype(BF)
    rows = dot(inner, wout_ref[0]).astype(BF)
    for k in range(parts):
        outs[k][...] = rows[k * cap : (k + 1) * cap, :]


def gather_rows(n, meta, ins, key_ref, gate_ref):
    key, gate = keys_of(meta, n)
    key_ref[...] = key
    gate_ref[...] = gate
    s = lax.axis_index("seq")
    cap = ins[0].shape[0]
    length = meta.shape[1]
    c = lax.broadcasted_iota(jnp.int32, (cap, length), 0).astype(F32)
    high, low = [], []
    for k in range(len(ins)):
        e = pl.ds(jnp.bitwise_xor(s, k), 1)
        w = jnp.where(c == key_ref[e, :], gate_ref[e, :], 0.0)
        h = w.astype(BF)
        high.append(h)
        low.append((w - h.astype(F32)).astype(BF))
    rows = jnp.concatenate([r[...] for r in ins], axis=0)
    dims = ((0,), (0,))
    return dot(jnp.concatenate(high, axis=0), rows, dims) + dot(jnp.concatenate(low, axis=0), rows, dims)


def partial_body(n, meta_ref, *refs):
    ins, out_ref, key_ref, gate_ref = refs[:-3], refs[-3], refs[-2], refs[-1]
    out_ref[...] = gather_rows(n, meta_ref[...], ins, key_ref, gate_ref).astype(BF)


def final_body(n, meta_ref, hidden_ref, other_ref, *refs):
    ins, out_ref, key_ref, gate_ref = refs[:-3], refs[-3], refs[-2], refs[-1]
    total = gather_rows(n, meta_ref[...], ins, key_ref, gate_ref)
    total = total + other_ref[...].astype(F32) + hidden_ref[...].astype(F32)
    out_ref[...] = total.astype(BF)


def small_group(
    queries,
    key_rows,
    value_rows,
    residual,
    out_weight,
    expert_in,
    expert_out,
    expert_ids,
    gate_values,
):
    n = lax.axis_size("seq")
    copies = lax.axis_size("win")
    length = queries.shape[0]
    y = lax.rem(lax.axis_index("seq"), 2)
    near = n // 2
    cap = max(2, 2 * length * TOP // n)
    half = H * DK // 2
    order = [2 * i for i in range(n // 2)] + [2 * i + 1 for i in reversed(range(n // 2))]
    ahead = [(order[i], order[(i + 1) % n]) for i in range(n)]
    back = [(b, a) for a, b in ahead]

    def flip(x, k):
        return lax.ppermute(x, "seq", [(i, i ^ k) for i in range(n)])

    def kernel(body, outs, xs, scratch=()):
        return call(body, outs, len(xs), scratch)(*xs)

    def flips(xs):
        return [xs[0]] + [flip(xs[k], k) for k in range(1, near)]

    offsets = [0]
    rows = H * DV // copies
    piece = lax.dynamic_slice_in_dim(out_weight, lax.axis_index("win") * rows, rows, 0)
    spread = []
    bit = copies // 2
    while bit:
        spread.append(bit)
        offsets = offsets + [o ^ bit for o in offsets]
        bit //= 2

    def share(x):
        held = [x]
        for k in spread:
            pairs = [(i, i ^ k) for i in range(copies)]
            held = held + [lax.ppermute(h, "win", pairs) for h in held]
        return held

    mine, sent = kernel(
        states_body,
        (sds((half, DV), F32), sds((half, DV), BF)),
        (key_rows, value_rows),
        [pltpu.VMEM((2 * half, DV), F32)],
    )
    got = flip(sent, 1).astype(F32)
    run = mine + got
    before = jnp.zeros_like(mine)
    step = 1
    while step < n // 2:
        hop = [(i, i + 2 * step) for i in range(n - 2 * step)]
        came = lax.ppermute(run.astype(BF), "seq", hop).astype(F32)
        before, run = before + came, run + came
        step *= 2
    prefix_mine = (before + jnp.where(y == 0, 0.0, got)).astype(BF)
    prefix_other = flip((before + jnp.where(y == 0, mine, 0.0)).astype(BF), 1)

    fs, bs = [], []
    f = b = piece
    for j in range(near):
        f = lax.ppermute(f, "seq", ahead)
        fs += share(f)
        if j < near - 1:
            b = lax.ppermute(b, "seq", back)
            bs += share(b)

    meta = jnp.concatenate([expert_ids.astype(F32), gate_values], axis=1).T
    meta_far = flip(meta, near)

    tokens = (queries, key_rows, value_rows)
    intra = [
        kernel(functools.partial(intra_body, i * (H // 4)), sds((length, H * DV // 2), F32), tokens)
        for i in range(2)
    ]
    row_buf = sds((cap, D), BF)
    full = sds((length, D), BF)
    keys = pltpu.VMEM((n, length), F32)
    hidden, normed, *deal_own = kernel(
        functools.partial(project_body, n, offsets),
        (full, full, *[row_buf] * near),
        (queries, *intra, prefix_mine, prefix_other, out_weight, residual, meta, *fs, *bs),
        [
            pltpu.VMEM((2 * half, DV), BF),
            pltpu.VMEM((length, H * DV), BF),
            pltpu.VMEM((length, D), F32),
            keys,
        ],
    )
    normed_far = flip(normed, near)
    own_in = flips(deal_own)
    deal_far = kernel(
        functools.partial(deal_body, n), tuple([row_buf] * near), (normed_far, meta_far), [keys]
    )
    far_in = flips(deal_far)

    def experts(xs):
        return kernel(
            functools.partial(expert_body, near),
            tuple([row_buf] * near),
            (expert_in, expert_out, *xs),
        )

    own_out = experts(own_in)
    own_back = flips(own_out)
    far_out = experts(far_in)
    far_back = flips(far_out)
    part_far = kernel(functools.partial(partial_body, n), full, (meta_far, *far_back), [keys, keys])
    part_own = flip(part_far, near)
    return kernel(
        functools.partial(final_body, n),
        jax.ShapeDtypeStruct((length, D), BF),
        (meta, hidden, part_own, *own_back),
        [keys, keys],
    )


def large_group(
    queries,
    key_rows,
    value_rows,
    residual,
    out_weight,
    expert_in,
    expert_out,
    expert_ids,
    gate_values,
):
    length = queries.shape[0]
    q_heads = queries.reshape(length, H, DK)
    k_heads = key_rows.reshape(length, H, DK)
    v_heads = value_rows.reshape(length, H, DV)
    local_state = jnp.einsum("thd,the->hde", k_heads, v_heads, preferred_element_type=F32)
    gathered = lax.all_gather(local_state.astype(BF), "seq")
    prefix = lax.fori_loop(
        0,
        lax.axis_index("seq"),
        lambda i, total: total + lax.dynamic_index_in_dim(gathered, i, 0, False).astype(F32),
        jnp.zeros_like(local_state),
    )
    causal = jnp.arange(length)[:, None] >= jnp.arange(length)[None, :]
    scores = jnp.einsum("thd,shd->hts", q_heads, k_heads, preferred_element_type=F32)
    scores = jnp.where(causal[None], scores, 0.0).astype(BF)
    intra_sum = jnp.einsum("hts,she->the", scores, v_heads, preferred_element_type=F32)
    inter_sum = jnp.einsum(
        "thd,hde->the", q_heads.astype(F32), prefix, precision=lax.Precision.HIGHEST
    )
    position = (lax.axis_index("seq") * length + jnp.arange(length)).astype(F32)
    scaling = lax.rsqrt((position + 1.0) * DK)
    attended = ((intra_sum + inter_sum) * scaling[:, None, None]).astype(BF).reshape(length, H * DV)
    projected = jnp.dot(
        attended,
        lax.all_gather(out_weight, "seq", axis=1, tiled=True),
        preferred_element_type=F32,
    )
    hidden = (residual.astype(F32) + projected).astype(BF)
    hidden_float = hidden.astype(F32)
    normed = (
        hidden_float
        * lax.rsqrt(jnp.mean(hidden_float * hidden_float, axis=-1, keepdims=True) + 1e-06)
    ).astype(BF)
    experts = lax.axis_size("seq") * expert_in.shape[0]
    capacity = max(2, 2 * length * TOP // experts)
    flat_ids = expert_ids.reshape(-1)
    one_hot = (flat_ids[:, None] == jnp.arange(experts)[None, :]).astype(jnp.int32)
    earlier = jnp.cumsum(one_hot, axis=0) - one_hot
    slot_index = jnp.sum(earlier * one_hot, axis=-1)
    dest_row = flat_ids * capacity + slot_index
    buffer = (
        jnp.zeros((experts * capacity, D), BF).at[dest_row].set(jnp.repeat(normed, TOP, axis=0))
    )
    buffer = buffer.reshape(experts, 1, capacity, D)
    act = jnp.einsum(
        "ensd,edf->ensf",
        lax.all_to_all(buffer, "seq", split_axis=0, concat_axis=1, tiled=True),
        expert_in,
        preferred_element_type=F32,
    )
    inner = (jax.nn.silu(act[..., :HE]) * act[..., HE:]).astype(BF)
    produced_all = jnp.einsum(
        "ensf,efd->ensd", inner, expert_out, preferred_element_type=F32
    ).astype(BF)
    returned_rows = lax.all_to_all(produced_all, "seq", split_axis=1, concat_axis=0, tiled=True)
    picked = returned_rows.reshape(experts * capacity, D)[dest_row]
    combined = jnp.sum(
        picked.astype(F32).reshape(length, TOP, D) * gate_values[:, :, None], axis=1
    )
    return (hidden_float + combined).astype(BF)


def solution(mesh):
    n = mesh.shape["seq"]
    even_win = mesh.shape["win"] % 2 == 0
    small = 4 <= n <= UNROLL_LIMIT and n & (n - 1) == 0 and even_win
    in_specs = (
        P(("win", "seq"), None),
        P(("win", "seq"), None),
        P(("win", "seq"), None),
        P(("win", "seq"), None),
        P(None, "seq"),
        P("seq", None, None),
        P("seq", None, None),
        P(("win", "seq"), None),
        P(("win", "seq"), None),
    )
    out_specs = P(("win", "seq"), None)
    if not small:
        return jax.shard_map(
            large_group, mesh=mesh, in_specs=in_specs, out_specs=out_specs, check_vma=False
        )

    return jax.shard_map(
        small_group, mesh=mesh, in_specs=in_specs, out_specs=out_specs, check_vma=False
    )
```

```python
import functools

import jax
import jax.numpy as jnp
from jax import lax
from jax.experimental import pallas as pl
from jax.experimental.pallas import tpu as pltpu
from jax.sharding import PartitionSpec as P


D = 1024
H = 16
DK = 64
DV = 128
HE = 384
TOP = 2
UNROLL_LIMIT = 16
KERNEL_VMEM = 24 * 1024 * 1024
BF = jnp.bfloat16
F32 = jnp.float32
VMEM = pl.BlockSpec(memory_space=pltpu.VMEM)


def call(body, outs, xs, scratch=(), in_hbm=()):
    run = pl.pallas_call(
        body,
        out_shape=outs,
        in_specs=[pl.BlockSpec(memory_space=pl.ANY) if i in in_hbm else VMEM for i in range(len(xs))],
        out_specs=jax.tree.map(lambda _: VMEM, outs),
        scratch_shapes=scratch,
        compiler_params=pltpu.CompilerParams(vmem_limit_bytes=KERNEL_VMEM),
    )
    spaces = [pltpu.HBM if i in in_hbm else pltpu.VMEM for i in range(len(xs))]
    return run(*[pltpu.with_memory_space_constraint(x, m) for x, m in zip(xs, spaces)])


def sds(shape, dtype):
    return pltpu.VMEM(shape, dtype)


def dot(a, b, dims=((1,), (0,))):
    return lax.dot_general(a, b, (dims, ((), ())), preferred_element_type=F32)


def states_body(k_ref, v_ref, ids_ref, gates_ref, w_ref, mine_ref, send_ref, meta_ref, piece_ref, full, sem):
    rows = piece_ref.shape[0]
    start = pl.multiple_of(lax.axis_index("win") * rows, rows)
    copy = pltpu.make_async_copy(w_ref.at[pl.ds(start, rows), :], piece_ref, sem)
    copy.start()
    meta_ref[0:TOP, :] = ids_ref[...].astype(F32)
    meta_ref[TOP : 2 * TOP, :] = gates_ref[...]
    half = full.shape[0] // 2
    for p in range(H // 2):
        r = dot(k_ref[:, 2 * DK * p : 2 * DK * (p + 1)], v_ref[:, 2 * DV * p : 2 * DV * (p + 1)], ((0,), (0,)))
        full[2 * DK * p : 2 * DK * p + DK, :] = r[:DK, :DV]
        full[2 * DK * p + DK : 2 * DK * (p + 1), :] = r[DK:, DV:]
    y = lax.rem(lax.axis_index("seq"), 2)
    mine_ref[...] = full[pl.ds(pl.multiple_of(y * half, half), half), :]
    send_ref[...] = full[pl.ds(pl.multiple_of((1 - y) * half, half), half), :].astype(BF)
    copy.wait()


def running_body(mine_ref, *refs):
    total = mine_ref[...]
    for r in refs[:-1]:
        total = total + r[...].astype(F32)
    refs[-1][...] = total.astype(BF)


def prefix_body(mine_ref, got_ref, *refs):
    came, own_ref, back_ref = refs[:-2], refs[-2], refs[-1]
    before = came[0][...].astype(F32)
    for r in came[1:]:
        before = before + r[...].astype(F32)
    even = lax.rem(lax.axis_index("seq"), 2) == 0
    got = got_ref[...].astype(F32)
    own_ref[...] = (before + jnp.where(even, jnp.zeros_like(got), got)).astype(BF)
    mine = mine_ref[...]
    back_ref[...] = (before + jnp.where(even, mine, jnp.zeros_like(mine))).astype(BF)


def pack_body(*refs):
    at = 0
    for r in refs[:-1]:
        refs[-1][at : at + r.shape[0], :] = r[...]
        at += r.shape[0]


def intra_body(first, q_ref, k_ref, v_ref, out_ref):
    length = q_ref.shape[0]
    lane = lax.broadcasted_iota(jnp.int32, (length, 2 * DK), 1)
    row = lax.broadcasted_iota(jnp.int32, (length, length), 0)
    col = lax.broadcasted_iota(jnp.int32, (length, length), 1)
    causal = row >= col
    for p in range(first, first + H // 4):
        q = q_ref[:, 2 * DK * p : 2 * DK * (p + 1)]
        k = k_ref[:, 2 * DK * p : 2 * DK * (p + 1)]
        for i in range(2):
            mine = (lane < DK) if i == 0 else (lane >= DK)
            s = dot(jnp.where(mine, q, jnp.zeros_like(q)), k, ((1,), (1,)))
            s = jnp.where(causal, s, 0.0).astype(BF)
            c = (2 * p + i) * DV
            o = c - 2 * first * DV
            out_ref[:, o : o + DV] = dot(s, v_ref[:, c : c + DV])


def keys_of(meta, experts):
    length = meta.shape[1]
    e = lax.broadcasted_iota(jnp.int32, (experts, length), 0).astype(F32)
    first, second = meta[0:1, :] == e, meta[1:2, :] == e
    named = jnp.logical_or(first, second)
    a = lax.broadcasted_iota(jnp.int32, (length, length), 0)
    b = lax.broadcasted_iota(jnp.int32, (length, length), 1)
    before = jnp.where(a < b, 1.0, 0.0).astype(BF)
    count = dot(jnp.where(named, 1.0, 0.0).astype(BF), before)
    key = jnp.where(named, count, -1.0)
    gate = jnp.where(first, meta[2:3, :], jnp.where(second, meta[3:4, :], 0.0))
    return key, gate


def deal(key_ref, normed, outs, cap):
    s = lax.axis_index("seq")
    length = normed.shape[0]
    c = lax.broadcasted_iota(jnp.int32, (cap, length), 0).astype(F32)
    picks = [
        jnp.where(c == key_ref[pl.ds(jnp.bitwise_xor(s, k), 1), :], 1.0, 0.0).astype(BF)
        for k in range(len(outs))
    ]
    rows = dot(jnp.concatenate(picks, axis=0), normed).astype(BF)
    for k, out in enumerate(outs):
        out[...] = rows[k * cap : (k + 1) * cap, :]


def project_body(n, offsets, groups, q_ref, ia_ref, ib_ref, pm_ref, po_ref, wown_ref, res_ref, meta_ref, *refs):
    copies = len(offsets)
    packs = [refs[g * copies : (g + 1) * copies] for g in range(len(groups))]
    refs = refs[len(groups) * copies :]
    hidden_ref, normed_ref = refs[:2]
    outs = refs[2 : 2 + n // 2]
    prefix, att, hid, key_ref = refs[2 + n // 2 :]
    s = lax.axis_index("seq")
    w = lax.axis_index("win")
    y = lax.rem(s, 2)
    length = q_ref.shape[0]
    half = prefix.shape[0] // 2
    prefix[pl.ds(pl.multiple_of(y * half, half), half), :] = pm_ref[...]
    prefix[pl.ds(pl.multiple_of((1 - y) * half, half), half), :] = po_ref[...]
    place = (s * length + lax.broadcasted_iota(jnp.int32, (length, 1), 0)).astype(F32)
    scaling = lax.rsqrt((place + 1.0) * DK)
    zero = jnp.zeros((DK, DV), BF)
    for p in range(H // 2):
        top = jnp.concatenate([prefix[2 * DK * p : 2 * DK * p + DK, :], zero], axis=1)
        low = jnp.concatenate([zero, prefix[2 * DK * p + DK : 2 * DK * (p + 1), :]], axis=1)
        inter = dot(q_ref[:, 2 * DK * p : 2 * DK * (p + 1)], jnp.concatenate([top, low], axis=0))
        cols = slice(2 * DV * p, 2 * DV * (p + 1))
        src, at = (ia_ref, p) if p < H // 4 else (ib_ref, p - H // 4)
        intra = src[:, 2 * DV * at : 2 * DV * (at + 1)]
        att[:, cols] = ((intra + inter) * scaling).astype(BF)
    rows = att.shape[1] // copies
    width = wown_ref.shape[1]
    parts = [
        att[:, pl.ds(pl.multiple_of(jnp.bitwise_xor(w, o) * rows, rows), rows)] for o in offsets
    ]
    pos = jnp.where(y == 0, s // 2, n - 1 - s // 2)

    def source(shift):
        at = lax.rem(pos + shift + n, n)
        return jnp.where(at < n // 2, 2 * at, 2 * (n - 1 - at) + 1)

    def put(shift, value):
        hid[:, pl.ds(pl.multiple_of(source(shift) * width, width), width)] = value

    put(0, dot(att[...], wown_ref[...]))
    for shifts, held in zip(groups, packs):
        for i in range(0, len(shifts), 2):
            some = shifts[i : i + 2]
            total = None
            for part, pack in zip(parts, held):
                m = [pack[(i + o) * rows : (i + o + 1) * rows, :] for o in range(len(some))]
                r = dot(part, jnp.concatenate(m, axis=1) if len(m) > 1 else m[0])
                total = r if total is None else total + r
            for o, shift in enumerate(some):
                put(shift, total[:, o * width : (o + 1) * width])
    hidden = (res_ref[...].astype(F32) + hid[...]).astype(BF)
    hidden_ref[...] = hidden
    h = hidden.astype(F32)
    normed = (h * lax.rsqrt(jnp.mean(h * h, axis=-1, keepdims=True) + 1e-06)).astype(BF)
    normed_ref[...] = normed
    key_ref[...] = keys_of(meta_ref[...], n)[0]
    deal(key_ref, normed, outs, outs[0].shape[0])


def deal_body(n, normed_ref, meta_ref, *refs):
    outs, key_ref = refs[:-1], refs[-1]
    key_ref[...] = keys_of(meta_ref[...], n)[0]
    deal(key_ref, normed_ref[...], outs, outs[0].shape[0])


def expert_body(parts, win_ref, wout_ref, *refs):
    ins, outs = refs[:parts], refs[parts:]
    cap = ins[0].shape[0]
    x = jnp.concatenate([r[...] for r in ins], axis=0)
    act = dot(x, win_ref[0])
    gate = act[:, :HE]
    inner = (gate / (1.0 + jnp.exp(-gate)) * act[:, HE:]).astype(BF)
    rows = dot(inner, wout_ref[0]).astype(BF)
    for k in range(parts):
        outs[k][...] = rows[k * cap : (k + 1) * cap, :]


def gather_rows(n, meta, ins, key_ref, gate_ref):
    key, gate = keys_of(meta, n)
    key_ref[...] = key
    gate_ref[...] = gate
    s = lax.axis_index("seq")
    cap = ins[0].shape[0]
    length = meta.shape[1]
    c = lax.broadcasted_iota(jnp.int32, (cap, length), 0).astype(F32)
    high, low = [], []
    for k in range(len(ins)):
        e = pl.ds(jnp.bitwise_xor(s, k), 1)
        w = jnp.where(c == key_ref[e, :], gate_ref[e, :], 0.0)
        h = w.astype(BF)
        high.append(h)
        low.append((w - h.astype(F32)).astype(BF))
    rows = jnp.concatenate([r[...] for r in ins], axis=0)
    dims = ((0,), (0,))
    return dot(jnp.concatenate(high, axis=0), rows, dims) + dot(jnp.concatenate(low, axis=0), rows, dims)


def partial_body(n, meta_ref, *refs):
    ins, out_ref, key_ref, gate_ref = refs[:-3], refs[-3], refs[-2], refs[-1]
    out_ref[...] = gather_rows(n, meta_ref[...], ins, key_ref, gate_ref).astype(BF)


def final_body(n, meta_ref, hidden_ref, other_ref, *refs):
    ins, out_ref, key_ref, gate_ref = refs[:-3], refs[-3], refs[-2], refs[-1]
    total = gather_rows(n, meta_ref[...], ins, key_ref, gate_ref)
    total = total + other_ref[...].astype(F32) + hidden_ref[...].astype(F32)
    out_ref[...] = total.astype(BF)


def small_group(
    queries,
    key_rows,
    value_rows,
    residual,
    out_weight,
    expert_in,
    expert_out,
    expert_ids,
    gate_values,
):
    n = lax.axis_size("seq")
    copies = lax.axis_size("win")
    length = queries.shape[0]
    y = lax.rem(lax.axis_index("seq"), 2)
    near = n // 2
    cap = max(2, 2 * length * TOP // n)
    half = H * DK // 2
    order = [2 * i for i in range(n // 2)] + [2 * i + 1 for i in reversed(range(n // 2))]
    ahead = [(order[i], order[(i + 1) % n]) for i in range(n)]
    back = [(b, a) for a, b in ahead]

    def flip(x, k):
        return lax.ppermute(x, "seq", [(i, i ^ k) for i in range(n)])

    def kernel(body, outs, xs, scratch=(), in_hbm=()):
        return call(body, outs, xs, scratch, in_hbm)

    def flips(xs):
        return [xs[0]] + [flip(xs[k], k) for k in range(1, near)]

    offsets = [0]
    rows = H * DV // copies
    spread = []
    bit = copies // 2
    while bit:
        spread.append(bit)
        offsets = offsets + [o ^ bit for o in offsets]
        bit //= 2

    def share(x):
        held = [x]
        for k in spread:
            pairs = [(i, i ^ k) for i in range(copies)]
            held = held + [lax.ppermute(h, "win", pairs) for h in held]
        return held

    width = out_weight.shape[1]
    mine, sent, meta, piece = kernel(
        states_body,
        (sds((half, DV), F32), sds((half, DV), BF), sds((2 * TOP, length), F32), sds((rows, width), BF)),
        (key_rows, value_rows, expert_ids.T, gate_values.T, out_weight),
        [pltpu.VMEM((2 * half, DV), F32), pltpu.SemaphoreType.DMA],
        in_hbm=(4,),
    )
    meta_far = flip(meta, near)
    state = sds((half, DV), BF)
    got = flip(sent, 1)
    came = []
    step = 1
    while step < n // 2:
        hop = [(i, i + 2 * step) for i in range(n - 2 * step)]
        run = kernel(running_body, state, (mine, got, *came))
        came.append(lax.ppermute(run, "seq", hop))
        step *= 2
    prefix_mine, prefix_back = kernel(prefix_body, (state, state), (mine, got, *came))
    prefix_other = flip(prefix_back, 1)

    fs, bs = [], []
    f = b = piece
    for j in range(near):
        f = lax.ppermute(f, "seq", ahead)
        fs.append(f)
        if j < near - 1:
            b = lax.ppermute(b, "seq", back)
            bs.append(b)
    steps = [[j] for j in range(near - 2)] + [[near - 2, near - 1]]
    groups, packs = [], []
    for js in steps:
        shifts, xs = [], []
        for j in js:
            shifts.append(-(j + 1))
            xs.append(fs[j])
            if j < near - 1:
                shifts.append(j + 1)
                xs.append(bs[j])
        groups.append(shifts)
        pack = kernel(pack_body, sds((rows * len(xs), width), BF), xs)
        packs += share(pack)

    tokens = (queries, key_rows, value_rows)
    intra = [
        kernel(functools.partial(intra_body, i * (H // 4)), sds((length, H * DV // 2), F32), tokens)
        for i in range(2)
    ]
    row_buf = sds((cap, D), BF)
    full = sds((length, D), BF)
    keys = pltpu.VMEM((n, length), F32)
    hidden, normed, *deal_own = kernel(
        functools.partial(project_body, n, offsets, groups),
        (full, full, *[row_buf] * near),
        (queries, *intra, prefix_mine, prefix_other, out_weight, residual, meta, *packs),
        [
            pltpu.VMEM((2 * half, DV), BF),
            pltpu.VMEM((length, H * DV), BF),
            pltpu.VMEM((length, D), F32),
            keys,
        ],
    )
    normed_far = flip(normed, near)
    own_in = flips(deal_own)
    deal_far = kernel(
        functools.partial(deal_body, n), tuple([row_buf] * near), (normed_far, meta_far), [keys]
    )
    far_in = flips(deal_far)

    def experts(xs):
        return kernel(
            functools.partial(expert_body, near),
            tuple([row_buf] * near),
            (expert_in, expert_out, *xs),
        )

    own_out = experts(own_in)
    own_back = flips(own_out)
    far_out = experts(far_in)
    far_back = flips(far_out)
    part_far = kernel(functools.partial(partial_body, n), full, (meta_far, *far_back), [keys, keys])
    part_own = flip(part_far, near)
    return kernel(
        functools.partial(final_body, n),
        jax.ShapeDtypeStruct((length, D), BF),
        (meta, hidden, part_own, *own_back),
        [keys, keys],
    )


def large_group(
    queries,
    key_rows,
    value_rows,
    residual,
    out_weight,
    expert_in,
    expert_out,
    expert_ids,
    gate_values,
):
    length = queries.shape[0]
    q_heads = queries.reshape(length, H, DK)
    k_heads = key_rows.reshape(length, H, DK)
    v_heads = value_rows.reshape(length, H, DV)
    local_state = jnp.einsum("thd,the->hde", k_heads, v_heads, preferred_element_type=F32)
    gathered = lax.all_gather(local_state.astype(BF), "seq")
    prefix = lax.fori_loop(
        0,
        lax.axis_index("seq"),
        lambda i, total: total + lax.dynamic_index_in_dim(gathered, i, 0, False).astype(F32),
        jnp.zeros_like(local_state),
    )
    causal = jnp.arange(length)[:, None] >= jnp.arange(length)[None, :]
    scores = jnp.einsum("thd,shd->hts", q_heads, k_heads, preferred_element_type=F32)
    scores = jnp.where(causal[None], scores, 0.0).astype(BF)
    intra_sum = jnp.einsum("hts,she->the", scores, v_heads, preferred_element_type=F32)
    inter_sum = jnp.einsum(
        "thd,hde->the", q_heads.astype(F32), prefix, precision=lax.Precision.HIGHEST
    )
    position = (lax.axis_index("seq") * length + jnp.arange(length)).astype(F32)
    scaling = lax.rsqrt((position + 1.0) * DK)
    attended = ((intra_sum + inter_sum) * scaling[:, None, None]).astype(BF).reshape(length, H * DV)
    projected = jnp.dot(
        attended,
        lax.all_gather(out_weight, "seq", axis=1, tiled=True),
        preferred_element_type=F32,
    )
    hidden = (residual.astype(F32) + projected).astype(BF)
    hidden_float = hidden.astype(F32)
    normed = (
        hidden_float
        * lax.rsqrt(jnp.mean(hidden_float * hidden_float, axis=-1, keepdims=True) + 1e-06)
    ).astype(BF)
    experts = lax.axis_size("seq") * expert_in.shape[0]
    capacity = max(2, 2 * length * TOP // experts)
    flat_ids = expert_ids.reshape(-1)
    one_hot = (flat_ids[:, None] == jnp.arange(experts)[None, :]).astype(jnp.int32)
    earlier = jnp.cumsum(one_hot, axis=0) - one_hot
    slot_index = jnp.sum(earlier * one_hot, axis=-1)
    dest_row = flat_ids * capacity + slot_index
    buffer = (
        jnp.zeros((experts * capacity, D), BF).at[dest_row].set(jnp.repeat(normed, TOP, axis=0))
    )
    buffer = buffer.reshape(experts, 1, capacity, D)
    act = jnp.einsum(
        "ensd,edf->ensf",
        lax.all_to_all(buffer, "seq", split_axis=0, concat_axis=1, tiled=True),
        expert_in,
        preferred_element_type=F32,
    )
    inner = (jax.nn.silu(act[..., :HE]) * act[..., HE:]).astype(BF)
    produced_all = jnp.einsum(
        "ensf,efd->ensd", inner, expert_out, preferred_element_type=F32
    ).astype(BF)
    returned_rows = lax.all_to_all(produced_all, "seq", split_axis=1, concat_axis=0, tiled=True)
    picked = returned_rows.reshape(experts * capacity, D)[dest_row]
    combined = jnp.sum(
        picked.astype(F32).reshape(length, TOP, D) * gate_values[:, :, None], axis=1
    )
    return (hidden_float + combined).astype(BF)


def solution(mesh):
    n = mesh.shape["seq"]
    even_win = mesh.shape["win"] % 2 == 0
    small = 4 <= n <= UNROLL_LIMIT and n & (n - 1) == 0 and even_win
    in_specs = (
        P(("win", "seq"), None),
        P(("win", "seq"), None),
        P(("win", "seq"), None),
        P(("win", "seq"), None),
        P(None, "seq"),
        P("seq", None, None),
        P("seq", None, None),
        P(("win", "seq"), None),
        P(("win", "seq"), None),
    )
    out_specs = P(("win", "seq"), None)
    if not small:
        return jax.shard_map(
            large_group, mesh=mesh, in_specs=in_specs, out_specs=out_specs, check_vma=False
        )

    return jax.shard_map(
        small_group, mesh=mesh, in_specs=in_specs, out_specs=out_specs, check_vma=False
    )
```

```python
import functools

import jax
import jax.numpy as jnp
from jax import lax
from jax.experimental import pallas as pl
from jax.experimental.pallas import tpu as pltpu
from jax.sharding import PartitionSpec as P


D = 1024
H = 16
DK = 64
DV = 128
HE = 384
TOP = 2
UNROLL_LIMIT = 16
KERNEL_VMEM = 24 * 1024 * 1024
BF = jnp.bfloat16
F32 = jnp.float32
VMEM = pl.BlockSpec(memory_space=pltpu.VMEM)


def call(body, outs, xs, scratch=(), in_hbm=(), loads=False):
    run = pl.pallas_call(
        body,
        out_shape=outs,
        in_specs=[pl.BlockSpec(memory_space=pl.ANY) if i in in_hbm else VMEM for i in range(len(xs))],
        out_specs=jax.tree.map(lambda _: VMEM, outs),
        scratch_shapes=scratch,
        compiler_params=pltpu.CompilerParams(vmem_limit_bytes=KERNEL_VMEM),
    )
    spaces = [pltpu.HBM if i in in_hbm or loads else pltpu.VMEM for i in range(len(xs))]
    return run(*[pltpu.with_memory_space_constraint(x, m) for x, m in zip(xs, spaces)])


def sds(shape, dtype):
    return pltpu.VMEM(shape, dtype)


def dot(a, b, dims=((1,), (0,))):
    return lax.dot_general(a, b, (dims, ((), ())), preferred_element_type=F32)


def states_body(k_ref, v_ref, ids_ref, gates_ref, w_ref, mine_ref, send_ref, meta_ref, piece_ref, full, sem):
    rows = piece_ref.shape[0]
    start = pl.multiple_of(lax.axis_index("win") * rows, rows)
    copy = pltpu.make_async_copy(w_ref.at[pl.ds(start, rows), :], piece_ref, sem)
    copy.start()
    meta_ref[0:TOP, :] = ids_ref[...].astype(F32)
    meta_ref[TOP : 2 * TOP, :] = gates_ref[...]
    half = full.shape[0] // 2
    for p in range(H // 2):
        r = dot(k_ref[:, 2 * DK * p : 2 * DK * (p + 1)], v_ref[:, 2 * DV * p : 2 * DV * (p + 1)], ((0,), (0,)))
        full[2 * DK * p : 2 * DK * p + DK, :] = r[:DK, :DV]
        full[2 * DK * p + DK : 2 * DK * (p + 1), :] = r[DK:, DV:]
    y = lax.rem(lax.axis_index("seq"), 2)
    mine_ref[...] = full[pl.ds(pl.multiple_of(y * half, half), half), :]
    send_ref[...] = full[pl.ds(pl.multiple_of((1 - y) * half, half), half), :].astype(BF)
    copy.wait()


def running_body(mine_ref, *refs):
    total = mine_ref[...]
    for r in refs[:-1]:
        total = total + r[...].astype(F32)
    refs[-1][...] = total.astype(BF)


def prefix_body(bits, mine_ref, got_ref, *refs):
    came, own_ref, back_ref = refs[:-2], refs[-2], refs[-1]
    s = lax.axis_index("seq")
    before = jnp.zeros(mine_ref.shape, F32)
    for bit, r in zip(bits, came):
        before = before + jnp.where(jnp.bitwise_and(s, bit) != 0, r[...].astype(F32), 0.0)
    even = jnp.bitwise_and(s, 1) == 0
    own_ref[...] = (before + jnp.where(even, 0.0, got_ref[...].astype(F32))).astype(BF)
    back_ref[...] = (before + jnp.where(even, mine_ref[...], 0.0)).astype(BF)


def pack_body(*refs):
    at = 0
    for r in refs[:-1]:
        refs[-1][at : at + r.shape[0], :] = r[...]
        at += r.shape[0]


def intra_body(first, q_ref, k_ref, v_ref, out_ref):
    length = q_ref.shape[0]
    lane = lax.broadcasted_iota(jnp.int32, (length, 2 * DK), 1)
    row = lax.broadcasted_iota(jnp.int32, (length, length), 0)
    col = lax.broadcasted_iota(jnp.int32, (length, length), 1)
    causal = row >= col
    for p in range(first, first + H // 4):
        q = q_ref[:, 2 * DK * p : 2 * DK * (p + 1)]
        k = k_ref[:, 2 * DK * p : 2 * DK * (p + 1)]
        for i in range(2):
            mine = (lane < DK) if i == 0 else (lane >= DK)
            s = dot(jnp.where(mine, q, jnp.zeros_like(q)), k, ((1,), (1,)))
            s = jnp.where(causal, s, 0.0).astype(BF)
            c = (2 * p + i) * DV
            o = c - 2 * first * DV
            out_ref[:, o : o + DV] = dot(s, v_ref[:, c : c + DV])


def keys_of(meta, experts):
    length = meta.shape[1]
    e = lax.broadcasted_iota(jnp.int32, (experts, length), 0).astype(F32)
    first, second = meta[0:1, :] == e, meta[1:2, :] == e
    named = jnp.logical_or(first, second)
    a = lax.broadcasted_iota(jnp.int32, (length, length), 0)
    b = lax.broadcasted_iota(jnp.int32, (length, length), 1)
    before = jnp.where(a < b, 1.0, 0.0).astype(BF)
    count = dot(jnp.where(named, 1.0, 0.0).astype(BF), before)
    key = jnp.where(named, count, -1.0)
    gate = jnp.where(first, meta[2:3, :], jnp.where(second, meta[3:4, :], 0.0))
    return key, gate


def deal(key_ref, normed, outs, cap):
    s = lax.axis_index("seq")
    length = normed.shape[0]
    c = lax.broadcasted_iota(jnp.int32, (cap, length), 0).astype(F32)
    picks = [
        jnp.where(c == key_ref[pl.ds(jnp.bitwise_xor(s, k), 1), :], 1.0, 0.0).astype(BF)
        for k in range(len(outs))
    ]
    rows = dot(jnp.concatenate(picks, axis=0), normed).astype(BF)
    for k, out in enumerate(outs):
        out[...] = rows[k * cap : (k + 1) * cap, :]


def project_body(n, offsets, groups, q_ref, ia_ref, ib_ref, pm_ref, po_ref, wown_ref, res_ref, meta_ref, *refs):
    copies = len(offsets)
    packs = [refs[g * copies : (g + 1) * copies] for g in range(len(groups))]
    refs = refs[len(groups) * copies :]
    hidden_ref, normed_ref = refs[:2]
    outs = refs[2 : 2 + n // 2]
    prefix, att, hid, key_ref = refs[2 + n // 2 :]
    s = lax.axis_index("seq")
    w = lax.axis_index("win")
    y = lax.rem(s, 2)
    length = q_ref.shape[0]
    half = prefix.shape[0] // 2
    prefix[pl.ds(pl.multiple_of(y * half, half), half), :] = pm_ref[...]
    prefix[pl.ds(pl.multiple_of((1 - y) * half, half), half), :] = po_ref[...]
    place = (s * length + lax.broadcasted_iota(jnp.int32, (length, 1), 0)).astype(F32)
    scaling = lax.rsqrt((place + 1.0) * DK)
    zero = jnp.zeros((DK, DV), BF)
    for p in range(H // 2):
        top = jnp.concatenate([prefix[2 * DK * p : 2 * DK * p + DK, :], zero], axis=1)
        low = jnp.concatenate([zero, prefix[2 * DK * p + DK : 2 * DK * (p + 1), :]], axis=1)
        inter = dot(q_ref[:, 2 * DK * p : 2 * DK * (p + 1)], jnp.concatenate([top, low], axis=0))
        cols = slice(2 * DV * p, 2 * DV * (p + 1))
        src, at = (ia_ref, p) if p < H // 4 else (ib_ref, p - H // 4)
        intra = src[:, 2 * DV * at : 2 * DV * (at + 1)]
        att[:, cols] = ((intra + inter) * scaling).astype(BF)
    rows = att.shape[1] // copies
    width = wown_ref.shape[1]
    parts = [
        att[:, pl.ds(pl.multiple_of(jnp.bitwise_xor(w, o) * rows, rows), rows)] for o in offsets
    ]
    pos = jnp.where(y == 0, s // 2, n - 1 - s // 2)

    def source(shift):
        at = lax.rem(pos + shift + n, n)
        return jnp.where(at < n // 2, 2 * at, 2 * (n - 1 - at) + 1)

    def put(shift, value):
        hid[:, pl.ds(pl.multiple_of(source(shift) * width, width), width)] = value

    put(0, dot(att[...], wown_ref[...]))
    for shifts, held in zip(groups, packs):
        for i in range(0, len(shifts), 2):
            some = shifts[i : i + 2]
            total = None
            for part, pack in zip(parts, held):
                m = [pack[(i + o) * rows : (i + o + 1) * rows, :] for o in range(len(some))]
                r = dot(part, jnp.concatenate(m, axis=1) if len(m) > 1 else m[0])
                total = r if total is None else total + r
            for o, shift in enumerate(some):
                put(shift, total[:, o * width : (o + 1) * width])
    hidden = (res_ref[...].astype(F32) + hid[...]).astype(BF)
    hidden_ref[...] = hidden
    h = hidden.astype(F32)
    normed = (h * lax.rsqrt(jnp.mean(h * h, axis=-1, keepdims=True) + 1e-06)).astype(BF)
    normed_ref[...] = normed
    key_ref[...] = keys_of(meta_ref[...], n)[0]
    deal(key_ref, normed, outs, outs[0].shape[0])


def deal_body(n, normed_ref, meta_ref, *refs):
    outs, key_ref = refs[:-1], refs[-1]
    key_ref[...] = keys_of(meta_ref[...], n)[0]
    deal(key_ref, normed_ref[...], outs, outs[0].shape[0])


def expert_body(parts, win_ref, wout_ref, *refs):
    ins, outs = refs[:parts], refs[parts:]
    cap = ins[0].shape[0]
    x = jnp.concatenate([r[...] for r in ins], axis=0)
    act = dot(x, win_ref[0])
    gate = act[:, :HE]
    inner = (gate / (1.0 + jnp.exp(-gate)) * act[:, HE:]).astype(BF)
    rows = dot(inner, wout_ref[0]).astype(BF)
    for k in range(parts):
        outs[k][...] = rows[k * cap : (k + 1) * cap, :]


def gather_rows(n, meta, ins, key_ref, gate_ref):
    key, gate = keys_of(meta, n)
    key_ref[...] = key
    gate_ref[...] = gate
    s = lax.axis_index("seq")
    cap = ins[0].shape[0]
    length = meta.shape[1]
    c = lax.broadcasted_iota(jnp.int32, (cap, length), 0).astype(F32)
    high, low = [], []
    for k in range(len(ins)):
        e = pl.ds(jnp.bitwise_xor(s, k), 1)
        w = jnp.where(c == key_ref[e, :], gate_ref[e, :], 0.0)
        h = w.astype(BF)
        high.append(h)
        low.append((w - h.astype(F32)).astype(BF))
    rows = jnp.concatenate([r[...] for r in ins], axis=0)
    dims = ((0,), (0,))
    return dot(jnp.concatenate(high, axis=0), rows, dims) + dot(jnp.concatenate(low, axis=0), rows, dims)


def partial_body(n, meta_ref, *refs):
    ins, out_ref, key_ref, gate_ref = refs[:-3], refs[-3], refs[-2], refs[-1]
    out_ref[...] = gather_rows(n, meta_ref[...], ins, key_ref, gate_ref).astype(BF)


def final_body(n, meta_ref, hidden_ref, other_ref, *refs):
    ins, out_ref, key_ref, gate_ref = refs[:-3], refs[-3], refs[-2], refs[-1]
    total = gather_rows(n, meta_ref[...], ins, key_ref, gate_ref)
    total = total + other_ref[...].astype(F32) + hidden_ref[...].astype(F32)
    out_ref[...] = total.astype(BF)


def small_group(
    queries,
    key_rows,
    value_rows,
    residual,
    out_weight,
    expert_in,
    expert_out,
    expert_ids,
    gate_values,
):
    n = lax.axis_size("seq")
    copies = lax.axis_size("win")
    length = queries.shape[0]
    y = lax.rem(lax.axis_index("seq"), 2)
    near = n // 2
    cap = max(2, 2 * length * TOP // n)
    half = H * DK // 2
    order = [2 * i for i in range(n // 2)] + [2 * i + 1 for i in reversed(range(n // 2))]
    ahead = [(order[i], order[(i + 1) % n]) for i in range(n)]
    back = [(b, a) for a, b in ahead]

    def flip(x, k):
        return lax.ppermute(x, "seq", [(i, i ^ k) for i in range(n)])

    def kernel(body, outs, xs, scratch=(), in_hbm=(), loads=False):
        return call(body, outs, xs, scratch, in_hbm, loads)

    def flips(xs):
        return [xs[0]] + [flip(xs[k], k) for k in range(1, near)]

    offsets = [0]
    rows = H * DV // copies
    spread = []
    bit = copies // 2
    while bit:
        spread.append(bit)
        offsets = offsets + [o ^ bit for o in offsets]
        bit //= 2

    def share(x):
        held = [x]
        for k in spread:
            pairs = [(i, i ^ k) for i in range(copies)]
            held = held + [lax.ppermute(h, "win", pairs) for h in held]
        return held

    width = out_weight.shape[1]
    mine, sent, meta, piece = kernel(
        states_body,
        (sds((half, DV), F32), sds((half, DV), BF), sds((2 * TOP, length), F32), sds((rows, width), BF)),
        (key_rows, value_rows, expert_ids.T, gate_values.T, out_weight),
        [pltpu.VMEM((2 * half, DV), F32), pltpu.SemaphoreType.DMA],
        in_hbm=(4,),
        loads=True,
    )
    meta_far = flip(meta, near)
    state = sds((half, DV), BF)
    got = flip(sent, 1)
    came, bits = [], []
    bit = 2
    while bit < n:
        run = kernel(running_body, state, (mine, got, *came))
        came.append(flip(run, bit))
        bits.append(bit)
        bit *= 2
    prefix_mine, prefix_back = kernel(
        functools.partial(prefix_body, bits), (state, state), (mine, got, *came)
    )
    prefix_other = flip(prefix_back, 1)

    fs, bs = [], []
    f = b = piece
    for j in range(near):
        f = lax.ppermute(f, "seq", ahead)
        fs.append(f)
        if j < near - 1:
            b = lax.ppermute(b, "seq", back)
            bs.append(b)
    steps = [[j] for j in range(near - 2)] + [[near - 2, near - 1]]
    groups, packs = [], []
    for js in steps:
        shifts, xs = [], []
        for j in js:
            shifts.append(-(j + 1))
            xs.append(fs[j])
            if j < near - 1:
                shifts.append(j + 1)
                xs.append(bs[j])
        groups.append(shifts)
        pack = kernel(pack_body, sds((rows * len(xs), width), BF), xs)
        packs += share(pack)

    tokens = (queries, key_rows, value_rows)
    intra = [
        kernel(functools.partial(intra_body, i * (H // 4)), sds((length, H * DV // 2), F32), tokens)
        for i in range(2)
    ]
    row_buf = sds((cap, D), BF)
    full = sds((length, D), BF)
    keys = pltpu.VMEM((n, length), F32)
    hidden, normed, *deal_own = kernel(
        functools.partial(project_body, n, offsets, groups),
        (full, full, *[row_buf] * near),
        (queries, *intra, prefix_mine, prefix_other, out_weight, residual, meta, *packs),
        [
            pltpu.VMEM((2 * half, DV), BF),
            pltpu.VMEM((length, H * DV), BF),
            pltpu.VMEM((length, D), F32),
            keys,
        ],
    )
    normed_far = flip(normed, near)
    own_in = flips(deal_own)
    deal_far = kernel(
        functools.partial(deal_body, n), tuple([row_buf] * near), (normed_far, meta_far), [keys]
    )
    far_in = flips(deal_far)

    def experts(xs):
        return kernel(
            functools.partial(expert_body, near),
            tuple([row_buf] * near),
            (expert_in, expert_out, *xs),
        )

    own_out = experts(own_in)
    own_back = flips(own_out)
    far_out = experts(far_in)
    far_back = flips(far_out)
    part_far = kernel(functools.partial(partial_body, n), full, (meta_far, *far_back), [keys, keys])
    part_own = flip(part_far, near)
    return kernel(
        functools.partial(final_body, n),
        jax.ShapeDtypeStruct((length, D), BF),
        (meta, hidden, part_own, *own_back),
        [keys, keys],
    )


def large_group(
    queries,
    key_rows,
    value_rows,
    residual,
    out_weight,
    expert_in,
    expert_out,
    expert_ids,
    gate_values,
):
    length = queries.shape[0]
    q_heads = queries.reshape(length, H, DK)
    k_heads = key_rows.reshape(length, H, DK)
    v_heads = value_rows.reshape(length, H, DV)
    local_state = jnp.einsum("thd,the->hde", k_heads, v_heads, preferred_element_type=F32)
    gathered = lax.all_gather(local_state.astype(BF), "seq")
    prefix = lax.fori_loop(
        0,
        lax.axis_index("seq"),
        lambda i, total: total + lax.dynamic_index_in_dim(gathered, i, 0, False).astype(F32),
        jnp.zeros_like(local_state),
    )
    causal = jnp.arange(length)[:, None] >= jnp.arange(length)[None, :]
    scores = jnp.einsum("thd,shd->hts", q_heads, k_heads, preferred_element_type=F32)
    scores = jnp.where(causal[None], scores, 0.0).astype(BF)
    intra_sum = jnp.einsum("hts,she->the", scores, v_heads, preferred_element_type=F32)
    inter_sum = jnp.einsum(
        "thd,hde->the", q_heads.astype(F32), prefix, precision=lax.Precision.HIGHEST
    )
    position = (lax.axis_index("seq") * length + jnp.arange(length)).astype(F32)
    scaling = lax.rsqrt((position + 1.0) * DK)
    attended = ((intra_sum + inter_sum) * scaling[:, None, None]).astype(BF).reshape(length, H * DV)
    projected = jnp.dot(
        attended,
        lax.all_gather(out_weight, "seq", axis=1, tiled=True),
        preferred_element_type=F32,
    )
    hidden = (residual.astype(F32) + projected).astype(BF)
    hidden_float = hidden.astype(F32)
    normed = (
        hidden_float
        * lax.rsqrt(jnp.mean(hidden_float * hidden_float, axis=-1, keepdims=True) + 1e-06)
    ).astype(BF)
    experts = lax.axis_size("seq") * expert_in.shape[0]
    capacity = max(2, 2 * length * TOP // experts)
    flat_ids = expert_ids.reshape(-1)
    one_hot = (flat_ids[:, None] == jnp.arange(experts)[None, :]).astype(jnp.int32)
    earlier = jnp.cumsum(one_hot, axis=0) - one_hot
    slot_index = jnp.sum(earlier * one_hot, axis=-1)
    dest_row = flat_ids * capacity + slot_index
    buffer = (
        jnp.zeros((experts * capacity, D), BF).at[dest_row].set(jnp.repeat(normed, TOP, axis=0))
    )
    buffer = buffer.reshape(experts, 1, capacity, D)
    act = jnp.einsum(
        "ensd,edf->ensf",
        lax.all_to_all(buffer, "seq", split_axis=0, concat_axis=1, tiled=True),
        expert_in,
        preferred_element_type=F32,
    )
    inner = (jax.nn.silu(act[..., :HE]) * act[..., HE:]).astype(BF)
    produced_all = jnp.einsum(
        "ensf,efd->ensd", inner, expert_out, preferred_element_type=F32
    ).astype(BF)
    returned_rows = lax.all_to_all(produced_all, "seq", split_axis=1, concat_axis=0, tiled=True)
    picked = returned_rows.reshape(experts * capacity, D)[dest_row]
    combined = jnp.sum(
        picked.astype(F32).reshape(length, TOP, D) * gate_values[:, :, None], axis=1
    )
    return (hidden_float + combined).astype(BF)


def solution(mesh):
    n = mesh.shape["seq"]
    even_win = mesh.shape["win"] % 2 == 0
    small = 4 <= n <= UNROLL_LIMIT and n & (n - 1) == 0 and even_win
    in_specs = (
        P(("win", "seq"), None),
        P(("win", "seq"), None),
        P(("win", "seq"), None),
        P(("win", "seq"), None),
        P(None, "seq"),
        P("seq", None, None),
        P("seq", None, None),
        P(("win", "seq"), None),
        P(("win", "seq"), None),
    )
    out_specs = P(("win", "seq"), None)
    if not small:
        return jax.shard_map(
            large_group, mesh=mesh, in_specs=in_specs, out_specs=out_specs, check_vma=False
        )

    return jax.shard_map(
        small_group, mesh=mesh, in_specs=in_specs, out_specs=out_specs, check_vma=False
    )
```

```python
import functools

import jax
import jax.numpy as jnp
from jax import lax
from jax.experimental import pallas as pl
from jax.experimental.pallas import tpu as pltpu
from jax.sharding import PartitionSpec as P


D = 1024
H = 16
DK = 64
DV = 128
HE = 384
TOP = 2
UNROLL_LIMIT = 16
KERNEL_VMEM = 24 * 1024 * 1024
BF = jnp.bfloat16
F32 = jnp.float32
VMEM = pl.BlockSpec(memory_space=pltpu.VMEM)


def call(body, outs, xs, scratch=(), in_hbm=(), loads=False):
    run = pl.pallas_call(
        body,
        out_shape=outs,
        in_specs=[pl.BlockSpec(memory_space=pl.ANY) if i in in_hbm else VMEM for i in range(len(xs))],
        out_specs=jax.tree.map(lambda _: VMEM, outs),
        scratch_shapes=scratch,
        compiler_params=pltpu.CompilerParams(vmem_limit_bytes=KERNEL_VMEM),
    )
    spaces = [pltpu.HBM if i in in_hbm or loads else pltpu.VMEM for i in range(len(xs))]
    return run(*[pltpu.with_memory_space_constraint(x, m) for x, m in zip(xs, spaces)])


def sds(shape, dtype):
    return pltpu.VMEM(shape, dtype)


def dot(a, b, dims=((1,), (0,))):
    return lax.dot_general(a, b, (dims, ((), ())), preferred_element_type=F32)


def states_body(k_ref, v_ref, ids_ref, gates_ref, w_ref, mine_ref, send_ref, meta_ref, piece_ref, full, sem):
    rows = piece_ref.shape[0]
    start = pl.multiple_of(lax.axis_index("win") * rows, rows)
    copy = pltpu.make_async_copy(w_ref.at[pl.ds(start, rows), :], piece_ref, sem)
    copy.start()
    meta_ref[0:TOP, :] = ids_ref[...].astype(F32)
    meta_ref[TOP : 2 * TOP, :] = gates_ref[...]
    half = full.shape[0] // 2
    for p in range(H // 2):
        r = dot(k_ref[:, 2 * DK * p : 2 * DK * (p + 1)], v_ref[:, 2 * DV * p : 2 * DV * (p + 1)], ((0,), (0,)))
        full[2 * DK * p : 2 * DK * p + DK, :] = r[:DK, :DV]
        full[2 * DK * p + DK : 2 * DK * (p + 1), :] = r[DK:, DV:]
    y = lax.rem(lax.axis_index("seq"), 2)
    mine_ref[...] = full[pl.ds(pl.multiple_of(y * half, half), half), :]
    send_ref[...] = full[pl.ds(pl.multiple_of((1 - y) * half, half), half), :].astype(BF)
    copy.wait()


def running_body(mine_ref, *refs):
    total = mine_ref[...]
    for r in refs[:-1]:
        total = total + r[...].astype(F32)
    refs[-1][...] = total.astype(BF)


def prefix_body(bits, mine_ref, got_ref, *refs):
    came, own_ref, back_ref = refs[:-2], refs[-2], refs[-1]
    s = lax.axis_index("seq")
    before = jnp.zeros(mine_ref.shape, F32)
    for bit, r in zip(bits, came):
        before = before + jnp.where(jnp.bitwise_and(s, bit) != 0, r[...].astype(F32), 0.0)
    even = jnp.bitwise_and(s, 1) == 0
    own_ref[...] = (before + jnp.where(even, 0.0, got_ref[...].astype(F32))).astype(BF)
    back_ref[...] = (before + jnp.where(even, mine_ref[...], 0.0)).astype(BF)


def pack_body(*refs):
    at = 0
    for r in refs[:-1]:
        refs[-1][at : at + r.shape[0], :] = r[...]
        at += r.shape[0]


def intra_body(first, q_ref, k_ref, v_ref, out_ref):
    length = q_ref.shape[0]
    lane = lax.broadcasted_iota(jnp.int32, (length, 2 * DK), 1)
    row = lax.broadcasted_iota(jnp.int32, (length, length), 0)
    col = lax.broadcasted_iota(jnp.int32, (length, length), 1)
    causal = row >= col
    for p in range(first, first + H // 4):
        q = q_ref[:, 2 * DK * p : 2 * DK * (p + 1)]
        k = k_ref[:, 2 * DK * p : 2 * DK * (p + 1)]
        for i in range(2):
            mine = (lane < DK) if i == 0 else (lane >= DK)
            s = dot(jnp.where(mine, q, jnp.zeros_like(q)), k, ((1,), (1,)))
            s = jnp.where(causal, s, 0.0).astype(BF)
            c = (2 * p + i) * DV
            o = c - 2 * first * DV
            out_ref[:, o : o + DV] = dot(s, v_ref[:, c : c + DV])


def keys_of(meta, experts):
    length = meta.shape[1]
    e = lax.broadcasted_iota(jnp.int32, (experts, length), 0).astype(F32)
    first, second = meta[0:1, :] == e, meta[1:2, :] == e
    named = jnp.logical_or(first, second)
    a = lax.broadcasted_iota(jnp.int32, (length, length), 0)
    b = lax.broadcasted_iota(jnp.int32, (length, length), 1)
    before = jnp.where(a < b, 1.0, 0.0).astype(BF)
    count = dot(jnp.where(named, 1.0, 0.0).astype(BF), before)
    key = jnp.where(named, count, -1.0)
    gate = jnp.where(first, meta[2:3, :], jnp.where(second, meta[3:4, :], 0.0))
    return key, gate


def deal(key_ref, normed, outs, cap):
    s = lax.axis_index("seq")
    length = normed.shape[0]
    c = lax.broadcasted_iota(jnp.int32, (cap, length), 0).astype(F32)
    picks = [
        jnp.where(c == key_ref[pl.ds(jnp.bitwise_xor(s, k), 1), :], 1.0, 0.0).astype(BF)
        for k in range(len(outs))
    ]
    rows = dot(jnp.concatenate(picks, axis=0), normed).astype(BF)
    for k, out in enumerate(outs):
        out[...] = rows[k * cap : (k + 1) * cap, :]


def column_of(n, s, shift):
    pos = jnp.where(jnp.bitwise_and(s, 1) == 0, s // 2, n - 1 - s // 2)
    at = lax.rem(pos + shift + n, n)
    return jnp.where(at < n // 2, 2 * at, 2 * (n - 1 - at) + 1)


def columns(n, s, shift, width):
    return pl.ds(pl.multiple_of(column_of(n, s, shift) * width, width), width)


def project_some(n, offsets, groups, packs, att, res_ref, out_ref, at):
    s = lax.axis_index("seq")
    w = lax.axis_index("win")
    rows = att.shape[1] // len(offsets)
    width = packs[0].shape[1]
    parts = [
        att[:, pl.ds(pl.multiple_of(jnp.bitwise_xor(w, o) * rows, rows), rows)] for o in offsets
    ]
    for g, shifts in enumerate(groups):
        held = packs[g * len(offsets) : (g + 1) * len(offsets)]
        for i in range(0, len(shifts), 2):
            some = shifts[i : i + 2]
            total = None
            for part, pack in zip(parts, held):
                m = [pack[(i + o) * rows : (i + o + 1) * rows, :] for o in range(len(some))]
                r = dot(part, jnp.concatenate(m, axis=1) if len(m) > 1 else m[0])
                total = r if total is None else total + r
            for o, shift in enumerate(some):
                value = total[:, o * width : (o + 1) * width]
                value = value + res_ref[:, columns(n, s, shift, width)].astype(F32)
                out_ref[:, at : at + width] = value.astype(BF)
                at += width


def early_body(n, offsets, groups, q_ref, ia_ref, ib_ref, pm_ref, po_ref, wown_ref, res_ref, *refs):
    packs, att, out_ref, prefix = refs[:-3], refs[-3], refs[-2], refs[-1]
    s = lax.axis_index("seq")
    y = lax.rem(s, 2)
    length = q_ref.shape[0]
    half = prefix.shape[0] // 2
    prefix[pl.ds(pl.multiple_of(y * half, half), half), :] = pm_ref[...]
    prefix[pl.ds(pl.multiple_of((1 - y) * half, half), half), :] = po_ref[...]
    place = (s * length + lax.broadcasted_iota(jnp.int32, (length, 1), 0)).astype(F32)
    scaling = lax.rsqrt((place + 1.0) * DK)
    zero = jnp.zeros((DK, DV), BF)
    for p in range(H // 2):
        top = jnp.concatenate([prefix[2 * DK * p : 2 * DK * p + DK, :], zero], axis=1)
        low = jnp.concatenate([zero, prefix[2 * DK * p + DK : 2 * DK * (p + 1), :]], axis=1)
        inter = dot(q_ref[:, 2 * DK * p : 2 * DK * (p + 1)], jnp.concatenate([top, low], axis=0))
        cols = slice(2 * DV * p, 2 * DV * (p + 1))
        src, at = (ia_ref, p) if p < H // 4 else (ib_ref, p - H // 4)
        intra = src[:, 2 * DV * at : 2 * DV * (at + 1)]
        att[:, cols] = ((intra + inter) * scaling).astype(BF)
    width = wown_ref.shape[1]
    own = dot(att[...], wown_ref[...]) + res_ref[:, columns(n, s, 0, width)].astype(F32)
    out_ref[:, :width] = own.astype(BF)
    project_some(n, offsets, groups, packs, att, res_ref, out_ref, width)


def assemble(n, s, shifts, first, second, hid):
    width = hid.shape[1] // n
    cut = first.shape[1] // width
    for i, shift in enumerate(shifts):
        src, at = (first, i) if i < cut else (second, i - cut)
        hid[:, columns(n, s, shift, width)] = src[:, at * width : (at + 1) * width].astype(F32)
    h = hid[...]
    return h, (h * lax.rsqrt(jnp.mean(h * h, axis=-1, keepdims=True) + 1e-06)).astype(BF)


def late_body(n, offsets, groups, shifts, att_ref, first_ref, res_ref, meta_ref, *refs):
    near = n // 2
    packs, refs = refs[: len(groups) * len(offsets)], refs[len(groups) * len(offsets) :]
    second_ref, hidden_ref = refs[:2]
    outs = refs[2 : 2 + near]
    hid, key_ref = refs[2 + near :]
    project_some(n, offsets, groups, packs, att_ref, res_ref, second_ref, 0)
    h, normed = assemble(n, lax.axis_index("seq"), shifts, first_ref, second_ref, hid)
    hidden_ref[...] = h.astype(BF)
    key_ref[...] = keys_of(meta_ref[...], n)[0]
    deal(key_ref, normed, outs, outs[0].shape[0])


def deal_body(n, shifts, first_ref, second_ref, meta_ref, *refs):
    outs, hid, key_ref = refs[:-2], refs[-2], refs[-1]
    key_ref[...] = keys_of(meta_ref[...], n)[0]
    sender = jnp.bitwise_xor(lax.axis_index("seq"), n // 2)
    normed = assemble(n, sender, shifts, first_ref, second_ref, hid)[1]
    deal(key_ref, normed, outs, outs[0].shape[0])


def expert_body(parts, win_ref, wout_ref, *refs):
    ins, outs = refs[:parts], refs[parts:]
    cap = ins[0].shape[0]
    x = jnp.concatenate([r[...] for r in ins], axis=0)
    act = dot(x, win_ref[0])
    gate = act[:, :HE]
    inner = (gate / (1.0 + jnp.exp(-gate)) * act[:, HE:]).astype(BF)
    rows = dot(inner, wout_ref[0]).astype(BF)
    for k in range(parts):
        outs[k][...] = rows[k * cap : (k + 1) * cap, :]


def gather_rows(n, meta, ins, key_ref, gate_ref):
    key, gate = keys_of(meta, n)
    key_ref[...] = key
    gate_ref[...] = gate
    s = lax.axis_index("seq")
    cap = ins[0].shape[0]
    length = meta.shape[1]
    c = lax.broadcasted_iota(jnp.int32, (cap, length), 0).astype(F32)
    high, low = [], []
    for k in range(len(ins)):
        e = pl.ds(jnp.bitwise_xor(s, k), 1)
        w = jnp.where(c == key_ref[e, :], gate_ref[e, :], 0.0)
        h = w.astype(BF)
        high.append(h)
        low.append((w - h.astype(F32)).astype(BF))
    rows = jnp.concatenate([r[...] for r in ins], axis=0)
    dims = ((0,), (0,))
    return dot(jnp.concatenate(high, axis=0), rows, dims) + dot(jnp.concatenate(low, axis=0), rows, dims)


def partial_body(n, meta_ref, *refs):
    ins, out_ref, key_ref, gate_ref = refs[:-3], refs[-3], refs[-2], refs[-1]
    out_ref[...] = gather_rows(n, meta_ref[...], ins, key_ref, gate_ref).astype(BF)


def final_body(n, meta_ref, hidden_ref, other_ref, *refs):
    ins, out_ref, key_ref, gate_ref = refs[:-3], refs[-3], refs[-2], refs[-1]
    total = gather_rows(n, meta_ref[...], ins, key_ref, gate_ref)
    total = total + other_ref[...].astype(F32) + hidden_ref[...].astype(F32)
    out_ref[...] = total.astype(BF)


def small_group(
    queries,
    key_rows,
    value_rows,
    residual,
    out_weight,
    expert_in,
    expert_out,
    expert_ids,
    gate_values,
):
    n = lax.axis_size("seq")
    copies = lax.axis_size("win")
    length = queries.shape[0]
    y = lax.rem(lax.axis_index("seq"), 2)
    near = n // 2
    cap = max(2, 2 * length * TOP // n)
    half = H * DK // 2
    order = [2 * i for i in range(n // 2)] + [2 * i + 1 for i in reversed(range(n // 2))]
    ahead = [(order[i], order[(i + 1) % n]) for i in range(n)]
    back = [(b, a) for a, b in ahead]

    def flip(x, k):
        return lax.ppermute(x, "seq", [(i, i ^ k) for i in range(n)])

    def kernel(body, outs, xs, scratch=(), in_hbm=(), loads=False):
        return call(body, outs, xs, scratch, in_hbm, loads)

    def flips(xs):
        return [xs[0]] + [flip(xs[k], k) for k in range(1, near)]

    offsets = [0]
    rows = H * DV // copies
    spread = []
    bit = copies // 2
    while bit:
        spread.append(bit)
        offsets = offsets + [o ^ bit for o in offsets]
        bit //= 2

    def share(x):
        held = [x]
        for k in spread:
            pairs = [(i, i ^ k) for i in range(copies)]
            held = held + [lax.ppermute(h, "win", pairs) for h in held]
        return held

    width = out_weight.shape[1]
    mine, sent, meta, piece = kernel(
        states_body,
        (sds((half, DV), F32), sds((half, DV), BF), sds((2 * TOP, length), F32), sds((rows, width), BF)),
        (key_rows, value_rows, expert_ids.T, gate_values.T, out_weight),
        [pltpu.VMEM((2 * half, DV), F32), pltpu.SemaphoreType.DMA],
        in_hbm=(4,),
        loads=True,
    )
    meta_far = flip(meta, near)
    state = sds((half, DV), BF)
    got = flip(sent, 1)
    came, bits = [], []
    bit = 2
    while bit < n:
        run = kernel(running_body, state, (mine, got, *came))
        came.append(flip(run, bit))
        bits.append(bit)
        bit *= 2
    prefix_mine, prefix_back = kernel(
        functools.partial(prefix_body, bits), (state, state), (mine, got, *came)
    )
    prefix_other = flip(prefix_back, 1)

    fs, bs = [], []
    f = b = piece
    for j in range(near):
        f = lax.ppermute(f, "seq", ahead)
        fs.append(f)
        if j < near - 1:
            b = lax.ppermute(b, "seq", back)
            bs.append(b)
    steps = [[j] for j in range(near - 2)] + [[near - 2, near - 1]]
    groups, packs = [], []
    for js in steps:
        shifts, xs = [], []
        for j in js:
            shifts.append(-(j + 1))
            xs.append(fs[j])
            if j < near - 1:
                shifts.append(j + 1)
                xs.append(bs[j])
        groups.append(shifts)
        pack = kernel(pack_body, sds((rows * len(xs), width), BF), xs)
        packs += share(pack)

    tokens = (queries, key_rows, value_rows)
    intra = [
        kernel(functools.partial(intra_body, i * (H // 4)), sds((length, H * DV // 2), F32), tokens)
        for i in range(2)
    ]
    row_buf = sds((cap, D), BF)
    full = sds((length, D), BF)
    keys = pltpu.VMEM((n, length), F32)
    early, late = groups[:-1], groups[-1:]
    ahead_packs, last_packs = packs[:-copies], packs[-copies:]
    shifts = [0] + [x for g in groups for x in g]
    left = len(groups[-1])
    some = sds((length, (n - left) * width), BF)
    rest = sds((length, left * width), BF)
    whole = pltpu.VMEM((length, D), F32)
    att, first = kernel(
        functools.partial(early_body, n, offsets, early),
        (sds((length, H * DV), BF), some),
        (queries, *intra, prefix_mine, prefix_other, out_weight, residual, *ahead_packs),
        [pltpu.VMEM((2 * half, DV), BF)],
    )
    first_far = flip(first, near)
    second, hidden, *deal_own = kernel(
        functools.partial(late_body, n, offsets, late, shifts),
        (rest, full, *[row_buf] * near),
        (att, first, residual, meta, *last_packs),
        [whole, keys],
    )
    second_far = flip(second, near)
    own_in = flips(deal_own)
    deal_far = kernel(
        functools.partial(deal_body, n, shifts),
        tuple([row_buf] * near),
        (first_far, second_far, meta_far),
        [whole, keys],
    )
    far_in = flips(deal_far)

    def experts(xs):
        return kernel(
            functools.partial(expert_body, near),
            tuple([row_buf] * near),
            (expert_in, expert_out, *xs),
        )

    own_out = experts(own_in)
    own_back = flips(own_out)
    far_out = experts(far_in)
    far_back = flips(far_out)
    part_far = kernel(functools.partial(partial_body, n), full, (meta_far, *far_back), [keys, keys])
    part_own = flip(part_far, near)
    return kernel(
        functools.partial(final_body, n),
        jax.ShapeDtypeStruct((length, D), BF),
        (meta, hidden, part_own, *own_back),
        [keys, keys],
    )


def large_group(
    queries,
    key_rows,
    value_rows,
    residual,
    out_weight,
    expert_in,
    expert_out,
    expert_ids,
    gate_values,
):
    length = queries.shape[0]
    q_heads = queries.reshape(length, H, DK)
    k_heads = key_rows.reshape(length, H, DK)
    v_heads = value_rows.reshape(length, H, DV)
    local_state = jnp.einsum("thd,the->hde", k_heads, v_heads, preferred_element_type=F32)
    gathered = lax.all_gather(local_state.astype(BF), "seq")
    prefix = lax.fori_loop(
        0,
        lax.axis_index("seq"),
        lambda i, total: total + lax.dynamic_index_in_dim(gathered, i, 0, False).astype(F32),
        jnp.zeros_like(local_state),
    )
    causal = jnp.arange(length)[:, None] >= jnp.arange(length)[None, :]
    scores = jnp.einsum("thd,shd->hts", q_heads, k_heads, preferred_element_type=F32)
    scores = jnp.where(causal[None], scores, 0.0).astype(BF)
    intra_sum = jnp.einsum("hts,she->the", scores, v_heads, preferred_element_type=F32)
    inter_sum = jnp.einsum(
        "thd,hde->the", q_heads.astype(F32), prefix, precision=lax.Precision.HIGHEST
    )
    position = (lax.axis_index("seq") * length + jnp.arange(length)).astype(F32)
    scaling = lax.rsqrt((position + 1.0) * DK)
    attended = ((intra_sum + inter_sum) * scaling[:, None, None]).astype(BF).reshape(length, H * DV)
    projected = jnp.dot(
        attended,
        lax.all_gather(out_weight, "seq", axis=1, tiled=True),
        preferred_element_type=F32,
    )
    hidden = (residual.astype(F32) + projected).astype(BF)
    hidden_float = hidden.astype(F32)
    normed = (
        hidden_float
        * lax.rsqrt(jnp.mean(hidden_float * hidden_float, axis=-1, keepdims=True) + 1e-06)
    ).astype(BF)
    experts = lax.axis_size("seq") * expert_in.shape[0]
    capacity = max(2, 2 * length * TOP // experts)
    flat_ids = expert_ids.reshape(-1)
    one_hot = (flat_ids[:, None] == jnp.arange(experts)[None, :]).astype(jnp.int32)
    earlier = jnp.cumsum(one_hot, axis=0) - one_hot
    slot_index = jnp.sum(earlier * one_hot, axis=-1)
    dest_row = flat_ids * capacity + slot_index
    buffer = (
        jnp.zeros((experts * capacity, D), BF).at[dest_row].set(jnp.repeat(normed, TOP, axis=0))
    )
    buffer = buffer.reshape(experts, 1, capacity, D)
    act = jnp.einsum(
        "ensd,edf->ensf",
        lax.all_to_all(buffer, "seq", split_axis=0, concat_axis=1, tiled=True),
        expert_in,
        preferred_element_type=F32,
    )
    inner = (jax.nn.silu(act[..., :HE]) * act[..., HE:]).astype(BF)
    produced_all = jnp.einsum(
        "ensf,efd->ensd", inner, expert_out, preferred_element_type=F32
    ).astype(BF)
    returned_rows = lax.all_to_all(produced_all, "seq", split_axis=1, concat_axis=0, tiled=True)
    picked = returned_rows.reshape(experts * capacity, D)[dest_row]
    combined = jnp.sum(
        picked.astype(F32).reshape(length, TOP, D) * gate_values[:, :, None], axis=1
    )
    return (hidden_float + combined).astype(BF)


def solution(mesh):
    n = mesh.shape["seq"]
    even_win = mesh.shape["win"] % 2 == 0
    small = 4 <= n <= UNROLL_LIMIT and n & (n - 1) == 0 and even_win
    in_specs = (
        P(("win", "seq"), None),
        P(("win", "seq"), None),
        P(("win", "seq"), None),
        P(("win", "seq"), None),
        P(None, "seq"),
        P("seq", None, None),
        P("seq", None, None),
        P(("win", "seq"), None),
        P(("win", "seq"), None),
    )
    out_specs = P(("win", "seq"), None)
    if not small:
        return jax.shard_map(
            large_group, mesh=mesh, in_specs=in_specs, out_specs=out_specs, check_vma=False
        )

    return jax.shard_map(
        small_group, mesh=mesh, in_specs=in_specs, out_specs=out_specs, check_vma=False
    )
```

```python
import functools

import jax
import jax.numpy as jnp
from jax import lax
from jax.experimental import pallas as pl
from jax.experimental.pallas import tpu as pltpu
from jax.sharding import PartitionSpec as P


D = 1024
H = 16
DK = 64
DV = 128
HE = 384
TOP = 2
UNROLL_LIMIT = 16
KERNEL_VMEM = 24 * 1024 * 1024
BF = jnp.bfloat16
F32 = jnp.float32
VMEM = pl.BlockSpec(memory_space=pltpu.VMEM)


def call(body, outs, xs, scratch=(), in_hbm=(), loads=False):
    run = pl.pallas_call(
        body,
        out_shape=outs,
        in_specs=[pl.BlockSpec(memory_space=pl.ANY) if i in in_hbm else VMEM for i in range(len(xs))],
        out_specs=jax.tree.map(lambda _: VMEM, outs),
        scratch_shapes=scratch,
        compiler_params=pltpu.CompilerParams(vmem_limit_bytes=KERNEL_VMEM),
    )
    spaces = [pltpu.HBM if i in in_hbm or loads else pltpu.VMEM for i in range(len(xs))]
    return run(*[pltpu.with_memory_space_constraint(x, m) for x, m in zip(xs, spaces)])


def sds(shape, dtype):
    return pltpu.VMEM(shape, dtype)


def dot(a, b, dims=((1,), (0,))):
    return lax.dot_general(a, b, (dims, ((), ())), preferred_element_type=F32)


def states_body(k_ref, v_ref, ids_ref, gates_ref, w_ref, mine_ref, send_ref, meta_ref, piece_ref, full, sem):
    rows = piece_ref.shape[0]
    start = pl.multiple_of(lax.axis_index("win") * rows, rows)
    copy = pltpu.make_async_copy(w_ref.at[pl.ds(start, rows), :], piece_ref, sem)
    copy.start()
    meta_ref[0:TOP, :] = ids_ref[...].astype(F32)
    meta_ref[TOP : 2 * TOP, :] = gates_ref[...]
    half = full.shape[0] // 2
    for p in range(H // 2):
        r = dot(k_ref[:, 2 * DK * p : 2 * DK * (p + 1)], v_ref[:, 2 * DV * p : 2 * DV * (p + 1)], ((0,), (0,)))
        full[2 * DK * p : 2 * DK * p + DK, :] = r[:DK, :DV]
        full[2 * DK * p + DK : 2 * DK * (p + 1), :] = r[DK:, DV:]
    y = lax.rem(lax.axis_index("seq"), 2)
    mine_ref[...] = full[pl.ds(pl.multiple_of(y * half, half), half), :]
    send_ref[...] = full[pl.ds(pl.multiple_of((1 - y) * half, half), half), :].astype(BF)
    copy.wait()


def running_body(mine_ref, *refs):
    total = mine_ref[...]
    for r in refs[:-1]:
        total = total + r[...].astype(F32)
    refs[-1][...] = total.astype(BF)


def prefix_body(bits, mine_ref, got_ref, *refs):
    came, own_ref, back_ref = refs[:-2], refs[-2], refs[-1]
    s = lax.axis_index("seq")
    before = jnp.zeros(mine_ref.shape, F32)
    for bit, r in zip(bits, came):
        before = before + jnp.where(jnp.bitwise_and(s, bit) != 0, r[...].astype(F32), 0.0)
    even = jnp.bitwise_and(s, 1) == 0
    own_ref[...] = (before + jnp.where(even, 0.0, got_ref[...].astype(F32))).astype(BF)
    back_ref[...] = (before + jnp.where(even, mine_ref[...], 0.0)).astype(BF)


def pack_body(*refs):
    at = 0
    for r in refs[:-1]:
        refs[-1][at : at + r.shape[0], :] = r[...]
        at += r.shape[0]


def intra_body(first, q_ref, k_ref, v_ref, out_ref):
    length = q_ref.shape[0]
    lane = lax.broadcasted_iota(jnp.int32, (length, 2 * DK), 1)
    row = lax.broadcasted_iota(jnp.int32, (length, length), 0)
    col = lax.broadcasted_iota(jnp.int32, (length, length), 1)
    causal = row >= col
    for p in range(first, first + H // 4):
        q = q_ref[:, 2 * DK * p : 2 * DK * (p + 1)]
        k = k_ref[:, 2 * DK * p : 2 * DK * (p + 1)]
        for i in range(2):
            mine = (lane < DK) if i == 0 else (lane >= DK)
            s = dot(jnp.where(mine, q, jnp.zeros_like(q)), k, ((1,), (1,)))
            s = jnp.where(causal, s, 0.0).astype(BF)
            c = (2 * p + i) * DV
            o = c - 2 * first * DV
            out_ref[:, o : o + DV] = dot(s, v_ref[:, c : c + DV])


def keys_of(meta, experts):
    length = meta.shape[1]
    e = lax.broadcasted_iota(jnp.int32, (experts, length), 0).astype(F32)
    first, second = meta[0:1, :] == e, meta[1:2, :] == e
    named = jnp.logical_or(first, second)
    a = lax.broadcasted_iota(jnp.int32, (length, length), 0)
    b = lax.broadcasted_iota(jnp.int32, (length, length), 1)
    before = jnp.where(a < b, 1.0, 0.0).astype(BF)
    count = dot(jnp.where(named, 1.0, 0.0).astype(BF), before)
    key = jnp.where(named, count, -1.0)
    gate = jnp.where(first, meta[2:3, :], jnp.where(second, meta[3:4, :], 0.0))
    return key, gate


def deal(key_ref, normed, outs, cap):
    s = lax.axis_index("seq")
    length = normed.shape[0]
    c = lax.broadcasted_iota(jnp.int32, (cap, length), 0).astype(F32)
    picks = [
        jnp.where(c == key_ref[pl.ds(jnp.bitwise_xor(s, k), 1), :], 1.0, 0.0).astype(BF)
        for k in range(len(outs))
    ]
    rows = dot(jnp.concatenate(picks, axis=0), normed).astype(BF)
    for k, out in enumerate(outs):
        out[...] = rows[k * cap : (k + 1) * cap, :]


def column_of(n, s, shift):
    pos = jnp.where(jnp.bitwise_and(s, 1) == 0, s // 2, n - 1 - s // 2)
    at = lax.rem(pos + shift + n, n)
    return jnp.where(at < n // 2, 2 * at, 2 * (n - 1 - at) + 1)


def columns(n, s, shift, width):
    return pl.ds(pl.multiple_of(column_of(n, s, shift) * width, width), width)


def project_some(n, offsets, groups, packs, att, res_ref, out_ref, at):
    s = lax.axis_index("seq")
    w = lax.axis_index("win")
    rows = att.shape[1] // len(offsets)
    width = packs[0].shape[1]
    parts = [
        att[:, pl.ds(pl.multiple_of(jnp.bitwise_xor(w, o) * rows, rows), rows)] for o in offsets
    ]
    for g, shifts in enumerate(groups):
        held = packs[g * len(offsets) : (g + 1) * len(offsets)]
        for i in range(0, len(shifts), 2):
            some = shifts[i : i + 2]
            total = None
            for part, pack in zip(parts, held):
                m = [pack[(i + o) * rows : (i + o + 1) * rows, :] for o in range(len(some))]
                r = dot(part, jnp.concatenate(m, axis=1) if len(m) > 1 else m[0])
                total = r if total is None else total + r
            for o, shift in enumerate(some):
                value = total[:, o * width : (o + 1) * width]
                value = value + res_ref[:, columns(n, s, shift, width)].astype(F32)
                out_ref[:, at : at + width] = value.astype(BF)
                at += width


def early_body(n, offsets, groups, q_ref, ia_ref, ib_ref, pm_ref, po_ref, wown_ref, res_ref, *refs):
    packs, att, out_ref, prefix = refs[:-3], refs[-3], refs[-2], refs[-1]
    s = lax.axis_index("seq")
    y = lax.rem(s, 2)
    length = q_ref.shape[0]
    half = prefix.shape[0] // 2
    prefix[pl.ds(pl.multiple_of(y * half, half), half), :] = pm_ref[...]
    prefix[pl.ds(pl.multiple_of((1 - y) * half, half), half), :] = po_ref[...]
    place = (s * length + lax.broadcasted_iota(jnp.int32, (length, 1), 0)).astype(F32)
    scaling = lax.rsqrt((place + 1.0) * DK)
    zero = jnp.zeros((DK, DV), BF)
    for p in range(H // 2):
        top = jnp.concatenate([prefix[2 * DK * p : 2 * DK * p + DK, :], zero], axis=1)
        low = jnp.concatenate([zero, prefix[2 * DK * p + DK : 2 * DK * (p + 1), :]], axis=1)
        inter = dot(q_ref[:, 2 * DK * p : 2 * DK * (p + 1)], jnp.concatenate([top, low], axis=0))
        cols = slice(2 * DV * p, 2 * DV * (p + 1))
        src, at = (ia_ref, p) if p < H // 4 else (ib_ref, p - H // 4)
        intra = src[:, 2 * DV * at : 2 * DV * (at + 1)]
        att[:, cols] = ((intra + inter) * scaling).astype(BF)
    width = wown_ref.shape[1]
    own = dot(att[...], wown_ref[...]) + res_ref[:, columns(n, s, 0, width)].astype(F32)
    out_ref[:, :width] = own.astype(BF)
    project_some(n, offsets, groups, packs, att, res_ref, out_ref, width)


def assemble(n, s, shifts, first, second, hid):
    width = hid.shape[1] // n
    cut = first.shape[1] // width
    for i, shift in enumerate(shifts):
        src, at = (first, i) if i < cut else (second, i - cut)
        hid[:, columns(n, s, shift, width)] = src[:, at * width : (at + 1) * width].astype(F32)
    h = hid[...]
    return h, (h * lax.rsqrt(jnp.mean(h * h, axis=-1, keepdims=True) + 1e-06)).astype(BF)


def late_body(n, offsets, groups, shifts, att_ref, first_ref, res_ref, meta_ref, *refs):
    near = n // 2
    packs, refs = refs[: len(groups) * len(offsets)], refs[len(groups) * len(offsets) :]
    second_ref, hidden_ref = refs[:2]
    outs = refs[2 : 2 + near]
    hid, key_ref = refs[2 + near :]
    project_some(n, offsets, groups, packs, att_ref, res_ref, second_ref, 0)
    h, normed = assemble(n, lax.axis_index("seq"), shifts, first_ref, second_ref, hid)
    hidden_ref[...] = h.astype(BF)
    key_ref[...] = keys_of(meta_ref[...], n)[0]
    deal(key_ref, normed, outs, outs[0].shape[0])


def deal_body(n, shifts, first_ref, second_ref, meta_ref, *refs):
    outs, hid, key_ref = refs[:-2], refs[-2], refs[-1]
    key_ref[...] = keys_of(meta_ref[...], n)[0]
    sender = jnp.bitwise_xor(lax.axis_index("seq"), n // 2)
    normed = assemble(n, sender, shifts, first_ref, second_ref, hid)[1]
    deal(key_ref, normed, outs, outs[0].shape[0])


def expert_body(parts, win_ref, wout_ref, *refs):
    ins, outs = refs[:parts], refs[parts:]
    cap = ins[0].shape[0]
    x = jnp.concatenate([r[...] for r in ins], axis=0)
    act = dot(x, win_ref[0])
    gate = act[:, :HE]
    inner = (gate / (1.0 + jnp.exp(-gate)) * act[:, HE:]).astype(BF)
    rows = dot(inner, wout_ref[0]).astype(BF)
    for k in range(parts):
        outs[k][...] = rows[k * cap : (k + 1) * cap, :]


def gather_rows(n, meta, ins, key_ref, gate_ref):
    key, gate = keys_of(meta, n)
    key_ref[...] = key
    gate_ref[...] = gate
    s = lax.axis_index("seq")
    cap = ins[0].shape[0]
    length = meta.shape[1]
    c = lax.broadcasted_iota(jnp.int32, (cap, length), 0).astype(F32)
    high, low = [], []
    for k in range(len(ins)):
        e = pl.ds(jnp.bitwise_xor(s, k), 1)
        w = jnp.where(c == key_ref[e, :], gate_ref[e, :], 0.0)
        h = w.astype(BF)
        high.append(h)
        low.append((w - h.astype(F32)).astype(BF))
    rows = jnp.concatenate([r[...] for r in ins], axis=0)
    dims = ((0,), (0,))
    return dot(jnp.concatenate(high, axis=0), rows, dims) + dot(jnp.concatenate(low, axis=0), rows, dims)


def partial_body(n, meta_ref, *refs):
    ins, out_ref, key_ref, gate_ref = refs[:-3], refs[-3], refs[-2], refs[-1]
    out_ref[...] = gather_rows(n, meta_ref[...], ins, key_ref, gate_ref).astype(BF)


def settle_body(n, meta_ref, hidden_ref, *refs):
    ins, out_ref, key_ref, gate_ref = refs[:-3], refs[-3], refs[-2], refs[-1]
    total = gather_rows(n, meta_ref[...], ins, key_ref, gate_ref)
    out_ref[...] = total + hidden_ref[...].astype(F32)


def final_body(total_ref, other_ref, out_ref):
    out_ref[...] = (total_ref[...] + other_ref[...].astype(F32)).astype(BF)


def small_group(
    queries,
    key_rows,
    value_rows,
    residual,
    out_weight,
    expert_in,
    expert_out,
    expert_ids,
    gate_values,
):
    n = lax.axis_size("seq")
    copies = lax.axis_size("win")
    length = queries.shape[0]
    y = lax.rem(lax.axis_index("seq"), 2)
    near = n // 2
    cap = max(2, 2 * length * TOP // n)
    half = H * DK // 2
    order = [2 * i for i in range(n // 2)] + [2 * i + 1 for i in reversed(range(n // 2))]
    ahead = [(order[i], order[(i + 1) % n]) for i in range(n)]
    back = [(b, a) for a, b in ahead]

    def flip(x, k):
        return lax.ppermute(x, "seq", [(i, i ^ k) for i in range(n)])

    def kernel(body, outs, xs, scratch=(), in_hbm=(), loads=False):
        return call(body, outs, xs, scratch, in_hbm, loads)

    def flips(xs):
        return [xs[0]] + [flip(xs[k], k) for k in range(1, near)]

    offsets = [0]
    rows = H * DV // copies
    spread = []
    bit = copies // 2
    while bit:
        spread.append(bit)
        offsets = offsets + [o ^ bit for o in offsets]
        bit //= 2

    def share(x):
        held = [x]
        for k in spread:
            pairs = [(i, i ^ k) for i in range(copies)]
            held = held + [lax.ppermute(h, "win", pairs) for h in held]
        return held

    width = out_weight.shape[1]
    mine, sent, meta, piece = kernel(
        states_body,
        (sds((half, DV), F32), sds((half, DV), BF), sds((2 * TOP, length), F32), sds((rows, width), BF)),
        (key_rows, value_rows, expert_ids.T, gate_values.T, out_weight),
        [pltpu.VMEM((2 * half, DV), F32), pltpu.SemaphoreType.DMA],
        in_hbm=(4,),
        loads=True,
    )
    meta_far = flip(meta, near)
    state = sds((half, DV), BF)
    got = flip(sent, 1)
    came, bits = [], []
    bit = 2
    while bit < n:
        run = kernel(running_body, state, (mine, got, *came))
        came.append(flip(run, bit))
        bits.append(bit)
        bit *= 2
    prefix_mine, prefix_back = kernel(
        functools.partial(prefix_body, bits), (state, state), (mine, got, *came)
    )
    prefix_other = flip(prefix_back, 1)

    fs, bs = [], []
    f = b = piece
    for j in range(near):
        f = lax.ppermute(f, "seq", ahead)
        fs.append(f)
        if j < near - 1:
            b = lax.ppermute(b, "seq", back)
            bs.append(b)
    steps = [[j] for j in range(near - 2)] + [[near - 2, near - 1]]
    groups, packs = [], []
    for js in steps:
        shifts, xs = [], []
        for j in js:
            shifts.append(-(j + 1))
            xs.append(fs[j])
            if j < near - 1:
                shifts.append(j + 1)
                xs.append(bs[j])
        groups.append(shifts)
        pack = kernel(pack_body, sds((rows * len(xs), width), BF), xs)
        packs += share(pack)

    tokens = (queries, key_rows, value_rows)
    intra = [
        kernel(functools.partial(intra_body, i * (H // 4)), sds((length, H * DV // 2), F32), tokens)
        for i in range(2)
    ]
    row_buf = sds((cap, D), BF)
    full = sds((length, D), BF)
    keys = pltpu.VMEM((n, length), F32)
    early, late = groups[:-1], groups[-1:]
    ahead_packs, last_packs = packs[:-copies], packs[-copies:]
    shifts = [0] + [x for g in groups for x in g]
    left = len(groups[-1])
    some = sds((length, (n - left) * width), BF)
    rest = sds((length, left * width), BF)
    whole = pltpu.VMEM((length, D), F32)
    att, first = kernel(
        functools.partial(early_body, n, offsets, early),
        (sds((length, H * DV), BF), some),
        (queries, *intra, prefix_mine, prefix_other, out_weight, residual, *ahead_packs),
        [pltpu.VMEM((2 * half, DV), BF)],
    )
    first_far = flip(first, near)
    second, hidden, *deal_own = kernel(
        functools.partial(late_body, n, offsets, late, shifts),
        (rest, full, *[row_buf] * near),
        (att, first, residual, meta, *last_packs),
        [whole, keys],
    )
    second_far = flip(second, near)
    own_in = flips(deal_own)
    deal_far = kernel(
        functools.partial(deal_body, n, shifts),
        tuple([row_buf] * near),
        (first_far, second_far, meta_far),
        [whole, keys],
    )
    far_in = flips(deal_far)

    def experts(xs):
        return kernel(
            functools.partial(expert_body, near),
            tuple([row_buf] * near),
            (expert_in, expert_out, *xs),
        )

    own_out = experts(own_in)
    own_back = flips(own_out)
    far_out = experts(far_in)
    far_back = flips(far_out)
    part_far = kernel(functools.partial(partial_body, n), full, (meta_far, *far_back), [keys, keys])
    part_own = flip(part_far, near)
    settled = kernel(
        functools.partial(settle_body, n),
        sds((length, D), F32),
        (meta, hidden, *own_back),
        [keys, keys],
    )
    return kernel(final_body, jax.ShapeDtypeStruct((length, D), BF), (settled, part_own))


def large_group(
    queries,
    key_rows,
    value_rows,
    residual,
    out_weight,
    expert_in,
    expert_out,
    expert_ids,
    gate_values,
):
    length = queries.shape[0]
    q_heads = queries.reshape(length, H, DK)
    k_heads = key_rows.reshape(length, H, DK)
    v_heads = value_rows.reshape(length, H, DV)
    local_state = jnp.einsum("thd,the->hde", k_heads, v_heads, preferred_element_type=F32)
    gathered = lax.all_gather(local_state.astype(BF), "seq")
    prefix = lax.fori_loop(
        0,
        lax.axis_index("seq"),
        lambda i, total: total + lax.dynamic_index_in_dim(gathered, i, 0, False).astype(F32),
        jnp.zeros_like(local_state),
    )
    causal = jnp.arange(length)[:, None] >= jnp.arange(length)[None, :]
    scores = jnp.einsum("thd,shd->hts", q_heads, k_heads, preferred_element_type=F32)
    scores = jnp.where(causal[None], scores, 0.0).astype(BF)
    intra_sum = jnp.einsum("hts,she->the", scores, v_heads, preferred_element_type=F32)
    inter_sum = jnp.einsum(
        "thd,hde->the", q_heads.astype(F32), prefix, precision=lax.Precision.HIGHEST
    )
    position = (lax.axis_index("seq") * length + jnp.arange(length)).astype(F32)
    scaling = lax.rsqrt((position + 1.0) * DK)
    attended = ((intra_sum + inter_sum) * scaling[:, None, None]).astype(BF).reshape(length, H * DV)
    projected = jnp.dot(
        attended,
        lax.all_gather(out_weight, "seq", axis=1, tiled=True),
        preferred_element_type=F32,
    )
    hidden = (residual.astype(F32) + projected).astype(BF)
    hidden_float = hidden.astype(F32)
    normed = (
        hidden_float
        * lax.rsqrt(jnp.mean(hidden_float * hidden_float, axis=-1, keepdims=True) + 1e-06)
    ).astype(BF)
    experts = lax.axis_size("seq") * expert_in.shape[0]
    capacity = max(2, 2 * length * TOP // experts)
    flat_ids = expert_ids.reshape(-1)
    one_hot = (flat_ids[:, None] == jnp.arange(experts)[None, :]).astype(jnp.int32)
    earlier = jnp.cumsum(one_hot, axis=0) - one_hot
    slot_index = jnp.sum(earlier * one_hot, axis=-1)
    dest_row = flat_ids * capacity + slot_index
    buffer = (
        jnp.zeros((experts * capacity, D), BF).at[dest_row].set(jnp.repeat(normed, TOP, axis=0))
    )
    buffer = buffer.reshape(experts, 1, capacity, D)
    act = jnp.einsum(
        "ensd,edf->ensf",
        lax.all_to_all(buffer, "seq", split_axis=0, concat_axis=1, tiled=True),
        expert_in,
        preferred_element_type=F32,
    )
    inner = (jax.nn.silu(act[..., :HE]) * act[..., HE:]).astype(BF)
    produced_all = jnp.einsum(
        "ensf,efd->ensd", inner, expert_out, preferred_element_type=F32
    ).astype(BF)
    returned_rows = lax.all_to_all(produced_all, "seq", split_axis=1, concat_axis=0, tiled=True)
    picked = returned_rows.reshape(experts * capacity, D)[dest_row]
    combined = jnp.sum(
        picked.astype(F32).reshape(length, TOP, D) * gate_values[:, :, None], axis=1
    )
    return (hidden_float + combined).astype(BF)


def solution(mesh):
    n = mesh.shape["seq"]
    even_win = mesh.shape["win"] % 2 == 0
    small = 4 <= n <= UNROLL_LIMIT and n & (n - 1) == 0 and even_win
    in_specs = (
        P(("win", "seq"), None),
        P(("win", "seq"), None),
        P(("win", "seq"), None),
        P(("win", "seq"), None),
        P(None, "seq"),
        P("seq", None, None),
        P("seq", None, None),
        P(("win", "seq"), None),
        P(("win", "seq"), None),
    )
    out_specs = P(("win", "seq"), None)
    if not small:
        return jax.shard_map(
            large_group, mesh=mesh, in_specs=in_specs, out_specs=out_specs, check_vma=False
        )

    return jax.shard_map(
        small_group, mesh=mesh, in_specs=in_specs, out_specs=out_specs, check_vma=False
    )
```

```python
import functools

import jax
import jax.numpy as jnp
from jax import lax
from jax.experimental import pallas as pl
from jax.experimental.pallas import tpu as pltpu
from jax.sharding import PartitionSpec as P


D = 1024
H = 16
DK = 64
DV = 128
HE = 384
TOP = 2
UNROLL_LIMIT = 16
KERNEL_VMEM = 24 * 1024 * 1024
BF = jnp.bfloat16
F32 = jnp.float32
VMEM = pl.BlockSpec(memory_space=pltpu.VMEM)


def call(body, outs, xs, scratch=(), in_hbm=(), loads=False):
    run = pl.pallas_call(
        body,
        out_shape=outs,
        in_specs=[pl.BlockSpec(memory_space=pl.ANY) if i in in_hbm else VMEM for i in range(len(xs))],
        out_specs=jax.tree.map(lambda _: VMEM, outs),
        scratch_shapes=scratch,
        compiler_params=pltpu.CompilerParams(vmem_limit_bytes=KERNEL_VMEM),
    )
    spaces = [pltpu.HBM if i in in_hbm or loads else pltpu.VMEM for i in range(len(xs))]
    return run(*[pltpu.with_memory_space_constraint(x, m) for x, m in zip(xs, spaces)])


def sds(shape, dtype):
    return pltpu.VMEM(shape, dtype)


def dot(a, b, dims=((1,), (0,))):
    return lax.dot_general(a, b, (dims, ((), ())), preferred_element_type=F32)


def states_body(
    other, k_ref, v_ref, ids_ref, gates_ref, w_ref, mine_ref, send_ref, meta_ref, piece_ref, extra_ref, full, sem
):
    rows = piece_ref.shape[0]
    w = lax.axis_index("win")
    copies = []
    for i, (part, dst) in enumerate(((w, piece_ref), (jnp.bitwise_xor(w, other), extra_ref))):
        start = pl.multiple_of(part * rows, rows)
        copies.append(pltpu.make_async_copy(w_ref.at[pl.ds(start, rows), :], dst, sem.at[i]))
    for copy in copies:
        copy.start()
    meta_ref[0:TOP, :] = ids_ref[...].astype(F32)
    meta_ref[TOP : 2 * TOP, :] = gates_ref[...]
    half = full.shape[0] // 2
    for p in range(H // 2):
        r = dot(k_ref[:, 2 * DK * p : 2 * DK * (p + 1)], v_ref[:, 2 * DV * p : 2 * DV * (p + 1)], ((0,), (0,)))
        full[2 * DK * p : 2 * DK * p + DK, :] = r[:DK, :DV]
        full[2 * DK * p + DK : 2 * DK * (p + 1), :] = r[DK:, DV:]
    y = lax.rem(lax.axis_index("seq"), 2)
    mine_ref[...] = full[pl.ds(pl.multiple_of(y * half, half), half), :]
    send_ref[...] = full[pl.ds(pl.multiple_of((1 - y) * half, half), half), :].astype(BF)
    for copy in copies:
        copy.wait()


def running_body(mine_ref, *refs):
    total = mine_ref[...]
    for r in refs[:-1]:
        total = total + r[...].astype(F32)
    refs[-1][...] = total.astype(BF)


def prefix_body(bits, mine_ref, got_ref, *refs):
    came, own_ref, back_ref = refs[:-2], refs[-2], refs[-1]
    s = lax.axis_index("seq")
    before = jnp.zeros(mine_ref.shape, F32)
    for bit, r in zip(bits, came):
        before = before + jnp.where(jnp.bitwise_and(s, bit) != 0, r[...].astype(F32), 0.0)
    even = jnp.bitwise_and(s, 1) == 0
    own_ref[...] = (before + jnp.where(even, 0.0, got_ref[...].astype(F32))).astype(BF)
    back_ref[...] = (before + jnp.where(even, mine_ref[...], 0.0)).astype(BF)


def pack_body(*refs):
    at = 0
    for r in refs[:-1]:
        refs[-1][at : at + r.shape[0], :] = r[...]
        at += r.shape[0]


def intra_body(first, q_ref, k_ref, v_ref, out_ref):
    length = q_ref.shape[0]
    lane = lax.broadcasted_iota(jnp.int32, (length, 2 * DK), 1)
    row = lax.broadcasted_iota(jnp.int32, (length, length), 0)
    col = lax.broadcasted_iota(jnp.int32, (length, length), 1)
    causal = row >= col
    for p in range(first, first + H // 4):
        q = q_ref[:, 2 * DK * p : 2 * DK * (p + 1)]
        k = k_ref[:, 2 * DK * p : 2 * DK * (p + 1)]
        for i in range(2):
            mine = (lane < DK) if i == 0 else (lane >= DK)
            s = dot(jnp.where(mine, q, jnp.zeros_like(q)), k, ((1,), (1,)))
            s = jnp.where(causal, s, 0.0).astype(BF)
            c = (2 * p + i) * DV
            o = c - 2 * first * DV
            out_ref[:, o : o + DV] = dot(s, v_ref[:, c : c + DV])


def keys_of(meta, experts):
    length = meta.shape[1]
    e = lax.broadcasted_iota(jnp.int32, (experts, length), 0).astype(F32)
    first, second = meta[0:1, :] == e, meta[1:2, :] == e
    named = jnp.logical_or(first, second)
    a = lax.broadcasted_iota(jnp.int32, (length, length), 0)
    b = lax.broadcasted_iota(jnp.int32, (length, length), 1)
    before = jnp.where(a < b, 1.0, 0.0).astype(BF)
    count = dot(jnp.where(named, 1.0, 0.0).astype(BF), before)
    key = jnp.where(named, count, -1.0)
    gate = jnp.where(first, meta[2:3, :], jnp.where(second, meta[3:4, :], 0.0))
    return key, gate


def deal(key_ref, normed, outs, cap):
    s = lax.axis_index("seq")
    length = normed.shape[0]
    c = lax.broadcasted_iota(jnp.int32, (cap, length), 0).astype(F32)
    picks = [
        jnp.where(c == key_ref[pl.ds(jnp.bitwise_xor(s, k), 1), :], 1.0, 0.0).astype(BF)
        for k in range(len(outs))
    ]
    rows = dot(jnp.concatenate(picks, axis=0), normed).astype(BF)
    for k, out in enumerate(outs):
        out[...] = rows[k * cap : (k + 1) * cap, :]


def column_of(n, s, shift):
    pos = jnp.where(jnp.bitwise_and(s, 1) == 0, s // 2, n - 1 - s // 2)
    at = lax.rem(pos + shift + n, n)
    return jnp.where(at < n // 2, 2 * at, 2 * (n - 1 - at) + 1)


def columns(n, s, shift, width):
    return pl.ds(pl.multiple_of(column_of(n, s, shift) * width, width), width)


def project_some(n, offsets, groups, packs, att, res_ref, out_ref, at):
    s = lax.axis_index("seq")
    w = lax.axis_index("win")
    rows = att.shape[1] // len(offsets)
    width = packs[0].shape[1]
    parts = [
        att[:, pl.ds(pl.multiple_of(jnp.bitwise_xor(w, o) * rows, rows), rows)] for o in offsets
    ]
    for g, shifts in enumerate(groups):
        held = packs[g * len(offsets) : (g + 1) * len(offsets)]
        for i in range(0, len(shifts), 2):
            some = shifts[i : i + 2]
            total = None
            for part, pack in zip(parts, held):
                m = [pack[(i + o) * rows : (i + o + 1) * rows, :] for o in range(len(some))]
                r = dot(part, jnp.concatenate(m, axis=1) if len(m) > 1 else m[0])
                total = r if total is None else total + r
            for o, shift in enumerate(some):
                value = total[:, o * width : (o + 1) * width]
                value = value + res_ref[:, columns(n, s, shift, width)].astype(F32)
                out_ref[:, at : at + width] = value.astype(BF)
                at += width


def early_body(n, offsets, groups, q_ref, ia_ref, ib_ref, pm_ref, po_ref, wown_ref, res_ref, meta_ref, *refs):
    packs, refs = refs[: len(groups) * len(offsets)], refs[len(groups) * len(offsets) :]
    att, out_ref = refs[:2]
    outs, prefix, key_ref = refs[2:-2], refs[-2], refs[-1]
    s = lax.axis_index("seq")
    y = lax.rem(s, 2)
    length = q_ref.shape[0]
    half = prefix.shape[0] // 2
    prefix[pl.ds(pl.multiple_of(y * half, half), half), :] = pm_ref[...]
    prefix[pl.ds(pl.multiple_of((1 - y) * half, half), half), :] = po_ref[...]
    place = (s * length + lax.broadcasted_iota(jnp.int32, (length, 1), 0)).astype(F32)
    scaling = lax.rsqrt((place + 1.0) * DK)
    zero = jnp.zeros((DK, DV), BF)
    for p in range(H // 2):
        top = jnp.concatenate([prefix[2 * DK * p : 2 * DK * p + DK, :], zero], axis=1)
        low = jnp.concatenate([zero, prefix[2 * DK * p + DK : 2 * DK * (p + 1), :]], axis=1)
        inter = dot(q_ref[:, 2 * DK * p : 2 * DK * (p + 1)], jnp.concatenate([top, low], axis=0))
        cols = slice(2 * DV * p, 2 * DV * (p + 1))
        src, at = (ia_ref, p) if p < H // 4 else (ib_ref, p - H // 4)
        intra = src[:, 2 * DV * at : 2 * DV * (at + 1)]
        att[:, cols] = ((intra + inter) * scaling).astype(BF)
    width = wown_ref.shape[1]
    own = dot(att[...], wown_ref[...]) + res_ref[:, columns(n, s, 0, width)].astype(F32)
    out_ref[:, :width] = own.astype(BF)
    project_some(n, offsets, groups, packs, att, res_ref, out_ref, width)
    key_ref[...] = keys_of(meta_ref[...], n)[0]
    deal(key_ref, out_ref[...], outs, outs[0].shape[0])


def assemble(n, s, shifts, first, second, out_ref, at):
    width = out_ref.shape[1] // n
    cut = first.shape[1] // width
    rows = first.shape[0]
    for i, shift in enumerate(shifts):
        src, j = (first, i) if i < cut else (second, i - cut)
        value = src[:, j * width : (j + 1) * width].astype(out_ref.dtype)
        out_ref[at : at + rows, columns(n, s, shift, width)] = value


def late_body(n, offsets, groups, att_ref, res_ref, meta_ref, *refs):
    packs, refs = refs[: len(groups) * len(offsets)], refs[len(groups) * len(offsets) :]
    out_ref, outs, key_ref = refs[0], refs[1:-1], refs[-1]
    project_some(n, offsets, groups, packs, att_ref, res_ref, out_ref, 0)
    key_ref[...] = keys_of(meta_ref[...], n)[0]
    deal(key_ref, out_ref[...], outs, outs[0].shape[0])


def deal_body(n, part_ref, meta_ref, *refs):
    outs, key_ref = refs[:-1], refs[-1]
    key_ref[...] = keys_of(meta_ref[...], n)[0]
    deal(key_ref, part_ref[...], outs, outs[0].shape[0])


def expert_body(n, shifts, sender, win_ref, wout_ref, *refs):
    near = n // 2
    firsts, seconds, outs, rows_ref = refs[:near], refs[near : 2 * near], refs[2 * near : 3 * near], refs[-1]
    cap = firsts[0].shape[0]
    s = lax.axis_index("seq")
    for k in range(near):
        owner = jnp.bitwise_xor(s, k ^ sender)
        assemble(n, owner, shifts, firsts[k], seconds[k], rows_ref, k * cap)
    h = rows_ref[...]
    x = (h * lax.rsqrt(jnp.mean(h * h, axis=-1, keepdims=True) + 1e-06)).astype(BF)
    act = dot(x, win_ref[0])
    gate = act[:, :HE]
    inner = (gate / (1.0 + jnp.exp(-gate)) * act[:, HE:]).astype(BF)
    rows = dot(inner, wout_ref[0]).astype(BF)
    for k in range(near):
        outs[k][...] = rows[k * cap : (k + 1) * cap, :]


def gather_rows(n, meta, ins, key_ref, gate_ref):
    key, gate = keys_of(meta, n)
    key_ref[...] = key
    gate_ref[...] = gate
    s = lax.axis_index("seq")
    cap = ins[0].shape[0]
    length = meta.shape[1]
    c = lax.broadcasted_iota(jnp.int32, (cap, length), 0).astype(F32)
    high, low = [], []
    for k in range(len(ins)):
        e = pl.ds(jnp.bitwise_xor(s, k), 1)
        w = jnp.where(c == key_ref[e, :], gate_ref[e, :], 0.0)
        h = w.astype(BF)
        high.append(h)
        low.append((w - h.astype(F32)).astype(BF))
    rows = jnp.concatenate([r[...] for r in ins], axis=0)
    dims = ((0,), (0,))
    return dot(jnp.concatenate(high, axis=0), rows, dims) + dot(jnp.concatenate(low, axis=0), rows, dims)


def partial_body(n, meta_ref, *refs):
    ins, out_ref, key_ref, gate_ref = refs[:-3], refs[-3], refs[-2], refs[-1]
    out_ref[...] = gather_rows(n, meta_ref[...], ins, key_ref, gate_ref).astype(BF)


def settle_body(n, shifts, meta_ref, first_ref, second_ref, *refs):
    ins, out_ref, hid, key_ref, gate_ref = refs[:-4], refs[-4], refs[-3], refs[-2], refs[-1]
    assemble(n, lax.axis_index("seq"), shifts, first_ref, second_ref, hid, 0)
    out_ref[...] = gather_rows(n, meta_ref[...], ins, key_ref, gate_ref) + hid[...]


def final_body(total_ref, other_ref, out_ref):
    out_ref[...] = (total_ref[...] + other_ref[...].astype(F32)).astype(BF)


def small_group(
    queries,
    key_rows,
    value_rows,
    residual,
    out_weight,
    expert_in,
    expert_out,
    expert_ids,
    gate_values,
):
    n = lax.axis_size("seq")
    copies = lax.axis_size("win")
    length = queries.shape[0]
    y = lax.rem(lax.axis_index("seq"), 2)
    near = n // 2
    cap = max(2, 2 * length * TOP // n)
    half = H * DK // 2
    order = [2 * i for i in range(n // 2)] + [2 * i + 1 for i in reversed(range(n // 2))]
    ahead = [(order[i], order[(i + 1) % n]) for i in range(n)]
    back = [(b, a) for a, b in ahead]

    def flip(x, k):
        return lax.ppermute(x, "seq", [(i, i ^ k) for i in range(n)])

    def kernel(body, outs, xs, scratch=(), in_hbm=(), loads=False):
        return call(body, outs, xs, scratch, in_hbm, loads)

    def flips(xs):
        return [xs[0]] + [flip(xs[k], k) for k in range(1, near)]

    offsets = [0]
    rows = H * DV // copies
    spread = []
    bit = copies // 2
    while bit:
        spread.append(bit)
        offsets = offsets + [o ^ bit for o in offsets]
        bit //= 2

    def share(held):
        for k in spread[len(held) - 1 :]:
            pairs = [(i, i ^ k) for i in range(copies)]
            held = held + [lax.ppermute(h, "win", pairs) for h in held]
        return held

    width = out_weight.shape[1]
    piece_buf = sds((rows, width), BF)
    mine, sent, meta, piece, extra = kernel(
        functools.partial(states_body, spread[0]),
        (sds((half, DV), F32), sds((half, DV), BF), sds((2 * TOP, length), F32), piece_buf, piece_buf),
        (key_rows, value_rows, expert_ids.T, gate_values.T, out_weight),
        [pltpu.VMEM((2 * half, DV), F32), pltpu.SemaphoreType.DMA((2,))],
        in_hbm=(4,),
        loads=True,
    )
    meta_far = flip(meta, near)
    state = sds((half, DV), BF)
    got = flip(sent, 1)
    came, bits = [], []
    bit = 2
    while bit < n:
        run = kernel(running_body, state, (mine, got, *came))
        came.append(flip(run, bit))
        bits.append(bit)
        bit *= 2
    prefix_mine, prefix_back = kernel(
        functools.partial(prefix_body, bits), (state, state), (mine, got, *came)
    )
    prefix_other = flip(prefix_back, 1)

    fs, bs = [], []
    f = b = piece
    for j in range(near):
        f = lax.ppermute(f, "seq", ahead)
        fs.append(f)
        if j < near - 1:
            b = lax.ppermute(b, "seq", back)
            bs.append(b)
    extra_f = lax.ppermute(extra, "seq", ahead)
    extra_b = lax.ppermute(extra, "seq", back)
    groups, packs = [], []
    for j in range(near):
        both = j < near - 1
        groups.append([-(j + 1), j + 1] if both else [-(j + 1)])
        if both:
            buf = sds((2 * rows, width), BF)
            held = [kernel(pack_body, buf, (fs[j], bs[j]))]
            if j == 0:
                held.append(kernel(pack_body, buf, (extra_f, extra_b)))
        else:
            held = [fs[j]]
        packs += share(held)

    tokens = (queries, key_rows, value_rows)
    intra = [
        kernel(functools.partial(intra_body, i * (H // 4)), sds((length, H * DV // 2), F32), tokens)
        for i in range(2)
    ]
    row_buf = sds((cap, D), BF)
    full = sds((length, D), BF)
    keys = pltpu.VMEM((n, length), F32)
    shifts = [0] + [x for g in groups for x in g]
    begun = near // 2
    done = 1 + sum(len(g) for g in groups[:begun])
    parts = (done * width, (n - done) * width)
    bufs = [[sds((cap, p), BF)] * near for p in parts]
    att, first, *own_a = kernel(
        functools.partial(early_body, n, offsets, groups[:begun]),
        (sds((length, H * DV), BF), sds((length, parts[0]), BF), *bufs[0]),
        (
            queries,
            *intra,
            prefix_mine,
            prefix_other,
            out_weight,
            residual,
            meta,
            *packs[: begun * copies],
        ),
        [pltpu.VMEM((2 * half, DV), BF), keys],
    )
    second, *own_b = kernel(
        functools.partial(late_body, n, offsets, groups[begun:]),
        (sds((length, parts[1]), BF), *bufs[1]),
        (att, residual, meta, *packs[begun * copies :]),
        [keys],
    )

    def dealt(x, i):
        return kernel(functools.partial(deal_body, n), tuple(bufs[i]), (x, meta_far), [keys])

    far_a = dealt(flip(first, near), 0)
    far_b = dealt(flip(second, near), 1)

    def experts(sender, xs):
        return kernel(
            functools.partial(expert_body, n, shifts, sender),
            tuple([row_buf] * near),
            (expert_in, expert_out, *xs),
            [pltpu.VMEM((near * cap, D), F32)],
        )

    own_out = experts(0, flips(own_a) + flips(own_b))
    far_out = experts(near, flips(far_a) + flips(far_b))
    own_back = flips(own_out)
    far_back = flips(far_out)
    part_far = kernel(functools.partial(partial_body, n), full, (meta_far, *far_back), [keys, keys])
    part_own = flip(part_far, near)
    settled = kernel(
        functools.partial(settle_body, n, shifts),
        sds((length, D), F32),
        (meta, first, second, *own_back),
        [pltpu.VMEM((length, D), F32), keys, keys],
    )
    return kernel(final_body, jax.ShapeDtypeStruct((length, D), BF), (settled, part_own))


def large_group(
    queries,
    key_rows,
    value_rows,
    residual,
    out_weight,
    expert_in,
    expert_out,
    expert_ids,
    gate_values,
):
    length = queries.shape[0]
    q_heads = queries.reshape(length, H, DK)
    k_heads = key_rows.reshape(length, H, DK)
    v_heads = value_rows.reshape(length, H, DV)
    local_state = jnp.einsum("thd,the->hde", k_heads, v_heads, preferred_element_type=F32)
    gathered = lax.all_gather(local_state.astype(BF), "seq")
    prefix = lax.fori_loop(
        0,
        lax.axis_index("seq"),
        lambda i, total: total + lax.dynamic_index_in_dim(gathered, i, 0, False).astype(F32),
        jnp.zeros_like(local_state),
    )
    causal = jnp.arange(length)[:, None] >= jnp.arange(length)[None, :]
    scores = jnp.einsum("thd,shd->hts", q_heads, k_heads, preferred_element_type=F32)
    scores = jnp.where(causal[None], scores, 0.0).astype(BF)
    intra_sum = jnp.einsum("hts,she->the", scores, v_heads, preferred_element_type=F32)
    inter_sum = jnp.einsum(
        "thd,hde->the", q_heads.astype(F32), prefix, precision=lax.Precision.HIGHEST
    )
    position = (lax.axis_index("seq") * length + jnp.arange(length)).astype(F32)
    scaling = lax.rsqrt((position + 1.0) * DK)
    attended = ((intra_sum + inter_sum) * scaling[:, None, None]).astype(BF).reshape(length, H * DV)
    projected = jnp.dot(
        attended,
        lax.all_gather(out_weight, "seq", axis=1, tiled=True),
        preferred_element_type=F32,
    )
    hidden = (residual.astype(F32) + projected).astype(BF)
    hidden_float = hidden.astype(F32)
    normed = (
        hidden_float
        * lax.rsqrt(jnp.mean(hidden_float * hidden_float, axis=-1, keepdims=True) + 1e-06)
    ).astype(BF)
    experts = lax.axis_size("seq") * expert_in.shape[0]
    capacity = max(2, 2 * length * TOP // experts)
    flat_ids = expert_ids.reshape(-1)
    one_hot = (flat_ids[:, None] == jnp.arange(experts)[None, :]).astype(jnp.int32)
    earlier = jnp.cumsum(one_hot, axis=0) - one_hot
    slot_index = jnp.sum(earlier * one_hot, axis=-1)
    dest_row = flat_ids * capacity + slot_index
    buffer = (
        jnp.zeros((experts * capacity, D), BF).at[dest_row].set(jnp.repeat(normed, TOP, axis=0))
    )
    buffer = buffer.reshape(experts, 1, capacity, D)
    act = jnp.einsum(
        "ensd,edf->ensf",
        lax.all_to_all(buffer, "seq", split_axis=0, concat_axis=1, tiled=True),
        expert_in,
        preferred_element_type=F32,
    )
    inner = (jax.nn.silu(act[..., :HE]) * act[..., HE:]).astype(BF)
    produced_all = jnp.einsum(
        "ensf,efd->ensd", inner, expert_out, preferred_element_type=F32
    ).astype(BF)
    returned_rows = lax.all_to_all(produced_all, "seq", split_axis=1, concat_axis=0, tiled=True)
    picked = returned_rows.reshape(experts * capacity, D)[dest_row]
    combined = jnp.sum(
        picked.astype(F32).reshape(length, TOP, D) * gate_values[:, :, None], axis=1
    )
    return (hidden_float + combined).astype(BF)


def solution(mesh):
    n = mesh.shape["seq"]
    even_win = mesh.shape["win"] % 2 == 0
    small = 4 <= n <= UNROLL_LIMIT and n & (n - 1) == 0 and even_win
    in_specs = (
        P(("win", "seq"), None),
        P(("win", "seq"), None),
        P(("win", "seq"), None),
        P(("win", "seq"), None),
        P(None, "seq"),
        P("seq", None, None),
        P("seq", None, None),
        P(("win", "seq"), None),
        P(("win", "seq"), None),
    )
    out_specs = P(("win", "seq"), None)
    if not small:
        return jax.shard_map(
            large_group, mesh=mesh, in_specs=in_specs, out_specs=out_specs, check_vma=False
        )

    return jax.shard_map(
        small_group, mesh=mesh, in_specs=in_specs, out_specs=out_specs, check_vma=False
    )
```
